32 devices in a mesh: dp: 8 (over z, y), mp: 4 (over x, core).
Axes of the slice: x: 2, y: 2, z: 4, core: 2. Of those that a mesh axis runs over, the one named last changes fastest.
Arguments:
- tokens: bfloat16 [16384, 768], P('dp'), may hold values from -6 to 6
- lengths: int32 [8, 2], P('dp'), may hold values from 0 to 2048, as said below
- mix_gain: float32 [768], replicated, may hold values from 0.5 to 1.5
- mix_shift: float32 [768], replicated, may hold values from -4 to 4
- proj_in: bfloat16 [768, 3, 768], P(None, None, 'mp'), may hold values from -0.21875 to 0.21875
- bias_in: float32 [3, 768], P(None, 'mp'), may hold values from -4 to 4
- short_taps: float32 [3, 3, 768], P(None, None, 'mp'), may hold values from -6 to 6
- long_taps: bfloat16 [2048, 768], P('dp', 'mp'), may hold values from -0.75 to 0.75
- decay_rates: float32 [768], P('mp'), may hold values from 0.00024414062 to 0.05
- skip_gain: float32 [768], P('mp'), may hold values from -6 to 6
- proj_out: bfloat16 [768, 768], P('mp'), may hold values from -0.21875 to 0.21875
- bias_out: float32 [768], replicated, may hold values from -4 to 4
- mlp_gain: float32 [768], replicated, may hold values from 0.5 to 1.5
- mlp_shift: float32 [768], replicated, may hold values from -4 to 4
- proj_up: bfloat16 [768, 3072], P(None, 'mp'), may hold values from -0.21875 to 0.21875
- bias_up: float32 [3072], P('mp'), may hold values from -4 to 4
- proj_down: bfloat16 [3072, 768], P('mp'), may hold values from -0.109375 to 0.109375
- bias_down: float32 [768], replicated, may hold values from -4 to 4
- cotangent: bfloat16 [16384, 768], P('dp'), may hold values from -6 to 6
Outputs:
- output: bfloat16 [16384, 768], P('dp')
- input_grad: float32 [16384, 768], P('dp')
- grad_mix_gain: float32 [768], replicated
- grad_mix_shift: float32 [768], replicated
- grad_proj_in: float32 [768, 3, 768], P(None, None, 'mp')
- grad_bias_in: float32 [3, 768], P(None, 'mp')
- grad_short_taps: float32 [3, 3, 768], P(None, None, 'mp')
- grad_long_taps: float32 [2048, 768], P('dp', 'mp')
- grad_decay_rates: float32 [768], P('mp')
- grad_skip_gain: float32 [768], P('mp')
- grad_proj_out: float32 [768, 768], P('mp')
- grad_bias_out: float32 [768], replicated
- grad_mlp_gain: float32 [768], replicated
- grad_mlp_shift: float32 [768], replicated
- grad_proj_up: float32 [768, 3072], P(None, 'mp')
- grad_bias_up: float32 [3072], P('mp')
- grad_proj_down: float32 [3072, 768], P('mp')
- grad_bias_down: float32 [768], replicated
The draws below stay inside these ranges and needn't reach their ends.
Inputs may be any that keep to these rules, and one draw needn't show every extreme that they name: Row g gives the lengths of the documents packed in order into group g's 2048 tokens: either one document of 2048 tokens and 0, or two of half of 2048 each; exactly half of the rows hold two documents.
All inputs are finite; a program needn't handle non-finite values.
Results may differ from the reference program's by a relative error of at most 0.024.
Values may be sent and summed in bfloat16 or wider, within the bound.
No kernel may reach another device: no remote copies, remote signals or barrier semaphores. Data moves between devices by JAX's collectives and lax.ppermute only.
A program may use at most 256 MiB of HBM per device.

```python
import math
import jax
import jax.numpy as jnp
from jax import lax

D = 768
FF = 3072
SEQ = 2048
GROUPS = 8
TOKENS = 16384
N_MP = 4


def draw_lengths(key, part):
    ordering = jax.random.permutation(key, GROUPS)
    halves = ordering < GROUPS // 2
    leading = jnp.where(halves, SEQ // 2, SEQ).astype(jnp.int32)
    return jnp.stack([leading, SEQ - leading], axis=1)


def shard_levels(rng, dims, split, least, largest):
    level = 1.0
    for dim, shards_of in split:
        steps = jax.random.uniform(jax.random.fold_in(jax.random.fold_in(rng, 6), dim), (shards_of,), jnp.float32, least / len(split), largest / len(split))
        level = level * jnp.repeat(jnp.exp(steps), dims[dim] // shards_of).reshape((-1,) + (1,) * (len(dims) - 1 - dim))
    return level


def gaussian(own_key, shape, deviation, reach, cuts=(), kind=jnp.bfloat16):
    factor_of = shard_levels(own_key, shape, cuts, -0.22, 0.18) if cuts else 1.0
    drawn = jax.random.normal(own_key, shape, jnp.float32) * deviation * factor_of
    return jnp.minimum(jnp.maximum(drawn, -reach), reach).astype(kind)


def setup_inputs(seed: int = 0) -> dict:
    streams_of = jax.random.split(jax.random.key(seed), 20)
    return {
        "tokens": gaussian(streams_of[0], (TOKENS, D), 1.0, 6.0, ((0, 8),)),
        "lengths": draw_lengths(jax.random.fold_in(streams_of[19], 71), 0),
        "mix_gain": jnp.clip(1.0 + 0.1 * jax.random.normal(streams_of[2], (D,), jnp.float32), 0.5, 1.5),
        "mix_shift": gaussian(streams_of[3], (D,), 0.3, 4.0, (), jnp.float32),
        "proj_in": gaussian(streams_of[4], (D, 3, D), D ** -0.5, 0.21875, ((2, 4),)),
        "bias_in": gaussian(streams_of[5], (3, D), 0.3, 4.0, ((1, 4),), jnp.float32),
        "short_taps": gaussian(streams_of[6], (3, 3, D), 0.6, 6.0, ((2, 4),), jnp.float32),
        "long_taps": gaussian(streams_of[7], (SEQ, D), 0.05, 0.75, ((0, 8), (1, 4))),
        "decay_rates": jnp.clip(jnp.exp(math.log(0.05) - 5.322034 * jax.random.uniform(streams_of[8], (D,), jnp.float32) ** shard_levels(streams_of[8], (D,), ((0, 4),), -0.2, 0.2)), 0.00024414062, 0.05),
        "skip_gain": gaussian(streams_of[9], (D,), 1.0, 6.0, ((0, 4),), jnp.float32),
        "proj_out": gaussian(streams_of[10], (D, D), D ** -0.5, 0.21875, ((0, 4),)),
        "bias_out": gaussian(streams_of[11], (D,), 0.3, 4.0, (), jnp.float32),
        "mlp_gain": jnp.clip(1.0 + 0.1 * jax.random.normal(streams_of[12], (D,), jnp.float32), 0.5, 1.5),
        "mlp_shift": gaussian(streams_of[13], (D,), 0.3, 4.0, (), jnp.float32),
        "proj_up": gaussian(streams_of[14], (D, FF), D ** -0.5, 0.21875, ((1, 4),)),
        "bias_up": gaussian(streams_of[15], (FF,), 0.3, 4.0, ((0, 4),), jnp.float32),
        "proj_down": gaussian(streams_of[16], (FF, D), FF ** -0.5, 0.109375, ((0, 4),)),
        "bias_down": gaussian(streams_of[17], (D,), 0.3, 4.0, (), jnp.float32),
        "cotangent": gaussian(streams_of[18], (TOKENS, D), 1.0, 6.0, ((0, 8),)),
    }


@jax.custom_vjp
def low(v):
    return lax.optimization_barrier(v.astype(jnp.bfloat16)).astype(jnp.float32)

@jax.custom_vjp
def low_back(v):
    return v

def low_keep(v):
    return (low(v), None)

def low_pass(kept, grad):
    return (grad,)

def back_keep(v):
    return (v, None)

def back_low(kept, grad):
    return (low(grad),)
low.defvjp(low_keep, low_pass)
low_back.defvjp(back_keep, back_low)

def layer_norm(values, scale_vec, shift_vec):
    average = lax.optimization_barrier(jnp.mean(values, axis=-1, keepdims=True))
    centered = values - average
    variance = lax.optimization_barrier(jnp.mean(centered * centered, axis=-1, keepdims=True))
    return centered * lax.rsqrt(variance + 1e-05) * scale_vec + shift_vec

def short_mix(first_len, streams, short_taps):
    seq_len = streams.shape[0]
    positions = jnp.arange(seq_len, dtype=jnp.int32)[:, None, None]
    result = short_taps[0] * streams
    for offset in (1, 2):
        shifted = jnp.concatenate([jnp.zeros((offset,) + streams.shape[1:], streams.dtype), streams[:-offset]], axis=0)
        valid_mask = (positions >= offset) & ((positions < first_len) | (positions - offset >= first_len))
        result = result + valid_mask.astype(streams.dtype) * (short_taps[offset] * shifted)
    return (result[:, 0], result[:, 1] * result[:, 2])

def build_kernel(raw_taps, decay_rates):
    seq_len = raw_taps.shape[0]
    positions = jnp.arange(seq_len).astype(raw_taps.dtype)[:, None]
    decayed = raw_taps * jnp.exp(-decay_rates * positions)
    padded = jnp.pad(decayed, ((1, 1), (0, 0)))
    pooled = (padded[:-2] + padded[1:-1] + padded[2:]) / 3.0
    return jnp.sign(pooled) * jnp.maximum(jnp.abs(pooled) - 0.003, 0.0)

def gate_mix(queries, conv_out, mixed_in, skip_gain):
    return queries * (conv_out + skip_gain * mixed_in)

def causal_conv(mixed_in, kernel, mask_one, mask_two):
    seq_len = mixed_in.shape[0]
    spectrum = jnp.fft.rfft(kernel, n=2 * seq_len, axis=0)
    totals = jnp.zeros_like(mixed_in)
    for doc_mask in (mask_one, mask_two):
        signal = jnp.fft.rfft(doc_mask * mixed_in, n=2 * seq_len, axis=0)
        totals = totals + doc_mask * jnp.fft.irfft(signal * spectrum, n=2 * seq_len, axis=0)[:seq_len]
    return totals

def grouped_sum(lhs_mat, rhs_mat):
    lhs_parts = lhs_mat.reshape(lhs_mat.shape[0], N_MP, -1)
    rhs_parts = rhs_mat.reshape(N_MP, -1, rhs_mat.shape[1])
    partial_sums = jnp.einsum('sgk,gkn->gsn', lhs_parts, rhs_parts, precision=lax.Precision.HIGHEST)
    return lax.optimization_barrier(jnp.sum(low(partial_sums), axis=0))

def grouped_columns(inputs, weight_three):
    copies = low_back(jnp.broadcast_to(inputs[None], (N_MP,) + inputs.shape))
    weight_parts = weight_three.reshape(weight_three.shape[0], weight_three.shape[1], N_MP, -1)
    result = jnp.einsum('gsd,djgk->sjgk', copies, weight_parts, precision=lax.Precision.HIGHEST)
    return result.reshape(inputs.shape[0], weight_three.shape[1], -1)

def block(params, token_rows, first_len, second_len):
    mix_gain, mix_shift, proj_in, bias_in, short_taps, long_taps, decay_rates, skip_gain, proj_out, bias_out, mlp_gain, mlp_shift, proj_up, bias_up, proj_down, bias_down = params
    seq_len = token_rows.shape[0]
    positions = jnp.arange(seq_len, dtype=jnp.int32)[:, None]
    mask_one = (positions < first_len).astype(token_rows.dtype)
    mask_two = ((positions >= first_len) & (positions < first_len + second_len)).astype(token_rows.dtype)
    normed = low(layer_norm(token_rows, mix_gain, mix_shift))
    streams = low_back(grouped_columns(normed, proj_in) + bias_in)
    queries, mixed_in = short_mix(first_len, streams, short_taps)
    kernel = build_kernel(long_taps, decay_rates)
    conv_out = causal_conv(mixed_in, kernel, mask_one, mask_two)
    gated_out = low(gate_mix(queries, conv_out, mixed_in, skip_gain))
    attn_out = low_back(grouped_sum(gated_out, proj_out)) + bias_out
    hidden_one = token_rows + attn_out
    normed_two = low(layer_norm(hidden_one, mlp_gain, mlp_shift))
    pre_act = low_back(grouped_columns(normed_two, proj_up[:, None, :])[:, 0] + bias_up)
    hidden = low(jax.nn.gelu(pre_act, approximate=False))
    return hidden_one + grouped_sum(hidden, proj_down) + bias_down

def reference(tokens, lengths, mix_gain, mix_shift, proj_in, bias_in, short_taps, long_taps, decay_rates, skip_gain, proj_out, bias_out, mlp_gain, mlp_shift, proj_up, bias_up, proj_down, bias_down, cotangent):
    params = tuple((weight.astype(jnp.float32) for weight in (mix_gain, mix_shift, proj_in, bias_in, short_taps, long_taps, decay_rates, skip_gain, proj_out, bias_out, mlp_gain, mlp_shift, proj_up, bias_up, proj_down, bias_down)))
    inputs = tokens.astype(jnp.float32).reshape(GROUPS, SEQ, D)
    cotangents = cotangent.astype(jnp.float32).reshape(GROUPS, SEQ, D)

    def one_group(running, item_row):
        group_tokens, group_cot, group_len = item_row

        def forward(values, weights):
            return block(weights, values, group_len[0], group_len[1])
        result, pullback = jax.vjp(forward, group_tokens, params)
        grad_tokens, grad_params = pullback(group_cot)
        summed = tuple((earlier + latest for earlier, latest in zip(running, grad_params)))
        return (summed, (result.astype(jnp.bfloat16), grad_tokens))
    start = tuple((jnp.zeros_like(weight) for weight in params))
    totals, (outputs, grads_in) = lax.scan(one_group, start, (inputs, cotangents, lengths))
    g_mix_gain, g_mix_shift, g_proj_in, g_bias_in, g_short, g_long, g_rates, g_skip, g_proj_out, g_bias_out, g_mlp_gain, g_mlp_shift, g_proj_up, g_bias_up, g_proj_down, g_bias_down = totals
    return (outputs.reshape(TOKENS, D), grads_in.reshape(TOKENS, D), g_mix_gain, g_mix_shift, g_proj_in, g_bias_in, g_short, g_long, g_rates, g_skip, g_proj_out, g_bias_out, g_mlp_gain, g_mlp_shift, g_proj_up, g_bias_up, g_proj_down, g_bias_down)
```

```python
from functools import partial
import math

import jax
import jax.numpy as jnp
import numpy as np
from jax import lax
from jax.experimental import pallas as pl
from jax.experimental.pallas import tpu as pltpu
from jax.sharding import PartitionSpec as P

F32 = jnp.float32
BF16 = jnp.bfloat16
EPS = 1e-05
CUT = 0.003
BLOCK = 128
SLAB = 16
TILE = 256
CHUNKS = 2
PAD = 8


def dot(lhs, rhs):
    return jnp.dot(lhs, rhs, preferred_element_type=F32)


def dot_rhs_t(lhs, rhs):
    return lax.dot_general(lhs, rhs, (((1,), (1,)), ((), ())), preferred_element_type=F32)


def dot_lhs_t(lhs, rhs):
    return lax.dot_general(lhs, rhs, (((0,), (0,)), ((), ())), preferred_element_type=F32)


def normalize(values):
    centered = values - jnp.mean(values, axis=-1, keepdims=True)
    rate = lax.rsqrt(jnp.mean(centered * centered, axis=-1, keepdims=True) + EPS)
    return centered * rate, rate


def norm_back(grad, unit, rate, gain):
    back = grad * gain
    mean_back = jnp.mean(back, axis=-1, keepdims=True)
    mean_unit = jnp.mean(back * unit, axis=-1, keepdims=True)
    return rate * (back - mean_back - unit * mean_unit)


def lane_parts(columns):
    return [(low, min(low + 128, columns)) for low in range(0, columns, 128)]


def whole(shape):
    zeros = (0,) * len(shape)
    return pl.BlockSpec(shape, lambda *_: zeros)


def fold_rows(values):
    rows, columns = values.shape
    return jnp.sum(values.reshape(rows // 8, 8, columns), axis=0)


def leaf_angles(count, angle):
    if count == 1:
        return [angle]
    return leaf_angles(count // 2, angle / 2) + leaf_angles(count // 2, angle / 2 + math.pi)


def split_tree(real, imag, angle):
    count = len(real)
    if count == 1:
        return [(real[0], imag[0])]
    half = count // 2
    cos, sin = math.cos(angle / 2), math.sin(angle / 2)
    plus, minus = ([], []), ([], [])
    for k in range(half):
        turned_re = cos * real[k + half] - sin * imag[k + half]
        turned_im = sin * real[k + half] + cos * imag[k + half]
        plus[0].append(real[k] + turned_re)
        plus[1].append(imag[k] + turned_im)
        minus[0].append(real[k] - turned_re)
        minus[1].append(imag[k] - turned_im)
    return split_tree(*plus, angle / 2) + split_tree(*minus, angle / 2 + math.pi)


def join_tree(leaves, angle):
    count = len(leaves)
    if count == 1:
        return [leaves[0][0]], [leaves[0][1]]
    half = count // 2
    cos, sin = math.cos(angle / 2), math.sin(angle / 2)
    plus = join_tree(leaves[:half], angle / 2)
    minus = join_tree(leaves[half:], angle / 2 + math.pi)
    low_re, low_im, high_re, high_im = [], [], [], []
    for k in range(half):
        diff_re = plus[0][k] - minus[0][k]
        diff_im = plus[1][k] - minus[1][k]
        low_re.append(plus[0][k] + minus[0][k])
        low_im.append(plus[1][k] + minus[1][k])
        high_re.append(cos * diff_re + sin * diff_im)
        high_im.append(cos * diff_im - sin * diff_re)
    return low_re + high_re, low_im + high_im


def tables(seq_len):
    count = seq_len // BLOCK
    angles = np.array(leaf_angles(count, math.pi / 2))
    index = np.arange(BLOCK)
    base = 2 * np.pi * np.outer(index, index) / BLOCK
    turn = np.outer(angles, index) / BLOCK
    rows = np.concatenate([np.cos(turn), np.sin(turn)], 0)
    columns = rows.T / seq_len
    return tuple(
        jnp.asarray(item.astype(np.float32)) for item in (np.cos(base), np.sin(base), rows, columns)
    )


def forward_table(tabs, leaf):
    cos_b, sin_b, rows, _ = tabs
    count = rows.shape[0] // 2
    cos_t = rows[leaf : leaf + 1, :]
    sin_t = rows[count + leaf : count + leaf + 1, :]
    cos = cos_b[...] * cos_t - sin_b[...] * sin_t
    sin = sin_b[...] * cos_t + cos_b[...] * sin_t
    top = jnp.concatenate([cos, -sin], axis=1)
    bottom = jnp.concatenate([sin, cos], axis=1)
    return jnp.concatenate([top, bottom], axis=0).astype(BF16)


def inverse_table(tabs, leaf):
    cos_b, sin_b, _, columns = tabs
    count = columns.shape[1] // 2
    cos_t = columns[:, leaf : leaf + 1]
    sin_t = columns[:, count + leaf : count + leaf + 1]
    cos = cos_b[...] * cos_t - sin_b[...] * sin_t
    sin = sin_b[...] * cos_t + cos_b[...] * sin_t
    top = jnp.concatenate([cos, sin], axis=1)
    bottom = jnp.concatenate([-sin, cos], axis=1)
    return jnp.concatenate([top, bottom], axis=0).astype(BF16)


def first_level(two_docs):
    one = jnp.where(two_docs, 0.0, 1.0).astype(F32)
    root = math.sqrt(0.5)
    signal = (root * one, root * one + (1.0 - one), 1.0 - 2.0 * one)
    filt = (root * one, root * one, 1.0 - 2.0 * one)
    return signal, filt


def blocks_in(load, level, count, columns, out_ref):
    cos, sin, sign = level
    half = count // 2

    def body(step, _):
        start = pl.multiple_of(step * SLAB, SLAB)
        for part in lane_parts(columns):
            lanes = slice(*part)
            items = [load(k, start, lanes) for k in range(count)]
            for branch in range(2):
                angle = math.pi / 4 + branch * math.pi
                c = cos * sign if branch else cos
                s = sin * sign if branch else sin
                real = [items[k] + c * items[k + half] for k in range(half)]
                imag = [s * items[k + half] for k in range(half)]
                leaves = split_tree(real, imag, angle)
                for leaf, (re, im) in enumerate(leaves):
                    where = branch * half + leaf
                    out_ref[where, pl.ds(start, SLAB), lanes] = re.astype(BF16)
                    out_ref[where, pl.ds(BLOCK + start, SLAB), lanes] = im.astype(BF16)
        return 0

    lax.fori_loop(0, BLOCK // SLAB, body, 0)


def blocks_out(store, level, count, columns, in_ref):
    cos, sin, sign = level
    half = count // 2

    def body(step, _):
        start = pl.multiple_of(step * SLAB, SLAB)
        for part in lane_parts(columns):
            lanes = slice(*part)
            joined = []
            for branch in range(2):
                leaves = []
                for leaf in range(half):
                    where = branch * half + leaf
                    leaves.append(
                        (
                            in_ref[where, pl.ds(start, SLAB), lanes],
                            in_ref[where, pl.ds(BLOCK + start, SLAB), lanes],
                        )
                    )
                joined.append(join_tree(leaves, math.pi / 4 + branch * math.pi))
            (plus_re, plus_im), (minus_re, minus_im) = joined
            for k in range(half):
                store(k, start, lanes, plus_re[k] + minus_re[k])
                high = cos * (plus_re[k] + sign * minus_re[k]) + sin * (
                    plus_im[k] + sign * minus_im[k]
                )
                store(k + half, start, lanes, high)
        return 0

    lax.fori_loop(0, BLOCK // SLAB, body, 0)


def complex_product(left, right, conjugate):
    l_re, l_im = left[:BLOCK], left[BLOCK:]
    r_re, r_im = right[:BLOCK], right[BLOCK:]
    if conjugate:
        real, imag = l_re * r_re + l_im * r_im, l_re * r_im - l_im * r_re
    else:
        real, imag = l_re * r_re - l_im * r_im, l_re * r_im + l_im * r_re
    return jnp.concatenate([real, imag], axis=0).astype(BF16)


def decay_taps(taps_ref, rates_ref, decayed_ref, decay_ref):
    seq_len, columns = taps_ref.shape
    pad = jnp.zeros((PAD, columns), F32)
    decayed_ref[0:PAD] = pad
    decayed_ref[PAD + seq_len :] = pad

    def body(step, _):
        start = pl.multiple_of(step * BLOCK, BLOCK)
        times = (lax.broadcasted_iota(jnp.int32, (BLOCK, columns), 0) + start).astype(F32)
        decay = jnp.exp(-rates_ref[...] * times)
        decayed_ref[pl.ds(PAD + start, BLOCK)] = taps_ref[pl.ds(start, BLOCK)].astype(F32) * decay
        if decay_ref is not None:
            decay_ref[pl.ds(start, BLOCK)] = decay
        return 0

    lax.fori_loop(0, seq_len // BLOCK, body, 0)


def three_sum(ref, row, size, lanes):
    window = ref[pl.ds(pl.multiple_of(row, 8), size + 2 * PAD), lanes]
    total = window[PAD - 1 : PAD - 1 + size] + window[PAD : PAD + size]
    return (total + window[PAD + 1 : PAD + 1 + size]) / 3.0


def mixer_in_kernel(
    flags, tok_ref, gain_ref, shift_ref, w_ref, b_ref, taps_ref,
    normed_ref, streams_ref, query_ref, pair_ref, mixed_ref, halo_ref,
):
    step = pl.program_id(0)
    tiles = pl.num_programs(0)
    rows = tok_ref.shape[0]
    unit, _ = normalize(tok_ref[...].astype(F32))
    normed = (unit * gain_ref[...] + shift_ref[...]).astype(BF16)
    normed_ref[...] = normed
    fresh = (step == 0) | ((flags[0] == 1) & (step * 2 == tiles))

    @pl.when(fresh)
    def _():
        halo_ref[:, 0:PAD] = jnp.zeros((3, PAD, halo_ref.shape[2]), F32)

    @pl.when(jnp.logical_not(fresh))
    def _():
        halo_ref[:, 0:PAD] = halo_ref[:, rows : rows + PAD]

    short = []
    for s in range(3):
        stream = dot(normed, w_ref[s]) + b_ref[s : s + 1]
        halo_ref[s, PAD:] = stream
        streams_ref[s] = stream.astype(BF16)
        short.append(
            taps_ref[s : s + 1] * stream
            + taps_ref[3 + s : 4 + s] * halo_ref[s, PAD - 1 : PAD - 1 + rows]
            + taps_ref[6 + s : 7 + s] * halo_ref[s, PAD - 2 : PAD - 2 + rows]
        )
    query_ref[...] = short[0].astype(BF16)
    pair_ref[0] = short[1].astype(BF16)
    pair_ref[1] = short[2].astype(BF16)
    mixed_ref[...] = short[1] * short[2]


def mixer_in(flags, tokens, gain, shift, w3, bias3, taps9):
    seq_len, width = tokens.shape
    channels = w3.shape[2]
    tiles = seq_len // TILE

    def rot(i, flags):
        return (lax.rem(i + flags[1] * (tiles // 2), tiles), 0)

    return pl.pallas_call(
        mixer_in_kernel,
        grid_spec=pltpu.PrefetchScalarGridSpec(
            num_scalar_prefetch=1,
            grid=(tiles,),
            in_specs=[
                pl.BlockSpec((TILE, width), lambda i, f: (i, 0)),
                whole((1, width)), whole((1, width)),
                whole(w3.shape), whole(bias3.shape), whole(taps9.shape),
            ],
            out_specs=[
                pl.BlockSpec((TILE, width), rot),
                pl.BlockSpec((3, TILE, channels), lambda i, f: (0, i, 0)),
                pl.BlockSpec((TILE, channels), lambda i, f: (i, 0)),
                pl.BlockSpec((2, TILE, channels), lambda i, f: (0, i, 0)),
                pl.BlockSpec((TILE, channels), lambda i, f: (i, 0)),
            ],
            scratch_shapes=[pltpu.VMEM((3, TILE + PAD, channels), F32)],
        ),
        out_shape=[
            jax.ShapeDtypeStruct((seq_len, width), BF16),
            jax.ShapeDtypeStruct((3, seq_len, channels), BF16),
            jax.ShapeDtypeStruct((seq_len, channels), BF16),
            jax.ShapeDtypeStruct((2, seq_len, channels), BF16),
            jax.ShapeDtypeStruct((seq_len, channels), F32),
        ],
        name="mixer_in",
        cost_estimate=pl.CostEstimate(
            flops=2 * seq_len * width * 3 * channels,
            bytes_accessed=seq_len * (width * 4 + channels * 18), transcendentals=0,
        ),
    )(flags, tokens, gain, shift, w3, bias3, taps9)


def conv_kernel(
    flags, mixed_ref, query_ref, taps_ref, rates_ref, skip_ref, *refs
):
    tabs, (gated_ref, arg_ref, xs_ref, ks_ref, decayed_ref, ax_ref, ak_ref, bb_ref) = (
        refs[:4], refs[4:]
    )
    seq_len, columns = mixed_ref.shape
    count = seq_len // BLOCK
    half_rows = seq_len // 2
    signal, filt = first_level(flags[0] == 1)
    decay_taps(taps_ref, rates_ref, decayed_ref, None)

    def load_mixed(k, start, lanes):
        return mixed_ref[pl.ds(k * BLOCK + start, SLAB), lanes]

    def load_taps(k, start, lanes):
        pooled = three_sum(decayed_ref, k * BLOCK + start, SLAB, lanes)
        return pooled - jnp.minimum(jnp.maximum(pooled, -CUT), CUT)

    blocks_in(load_mixed, signal, count, columns, ax_ref)
    blocks_in(load_taps, filt, count, columns, ak_ref)
    for leaf in range(count):
        table = forward_table(tabs, leaf)
        xs = dot(table, ax_ref[leaf])
        ks = dot(table, ak_ref[leaf])
        xs_ref[leaf] = xs.astype(BF16)
        ks_ref[leaf] = ks.astype(BF16)
        bb_ref[leaf] = dot(inverse_table(tabs, leaf), complex_product(ks, xs, False))
    bases = (flags[1] * half_rows, (1 - flags[1]) * half_rows)

    def store(k, start, lanes, value):
        rows = pl.ds(k * BLOCK + start, SLAB)
        arg = value + skip_ref[:, lanes] * mixed_ref[rows, lanes]
        arg_ref[rows, lanes] = arg.astype(BF16)
        gated = (query_ref[rows, lanes].astype(F32) * arg).astype(BF16)
        side, inner = divmod(k, count // 2)
        target = pl.multiple_of(bases[side] + inner * BLOCK + start, SLAB)
        gated_ref[pl.ds(target, SLAB), lanes] = gated

    blocks_out(store, signal, count, columns, bb_ref)


def conv_forward(flags, mixed, query, taps, rates, skip, tabs):
    seq_len, channels = mixed.shape
    count = seq_len // BLOCK
    args = (mixed, query, taps, rates, skip) + tabs
    spectrum = (count, 2 * BLOCK, channels)
    outs = [
        jax.ShapeDtypeStruct((seq_len, channels), BF16),
        jax.ShapeDtypeStruct((seq_len, channels), BF16),
        jax.ShapeDtypeStruct(spectrum, BF16),
        jax.ShapeDtypeStruct(spectrum, BF16),
    ]
    return pl.pallas_call(
        conv_kernel,
        grid_spec=pltpu.PrefetchScalarGridSpec(
            num_scalar_prefetch=1,
            grid=(1,),
            in_specs=[whole(item.shape) for item in args],
            out_specs=[whole(item.shape) for item in outs],
            scratch_shapes=[
                pltpu.VMEM((seq_len + 2 * PAD, channels), F32),
                pltpu.VMEM(spectrum, BF16),
                pltpu.VMEM(spectrum, BF16),
                pltpu.VMEM(spectrum, F32),
            ],
        ),
        out_shape=outs,
        name="conv_forward",
        cost_estimate=pl.CostEstimate(
            flops=2 * 3 * count * (2 * BLOCK) ** 2 * channels,
            bytes_accessed=seq_len * channels * 16, transcendentals=seq_len * channels,
        ),
    )(flags, *args)


def conv_back_kernel(
    flags, own_ref, other_ref, query_ref, arg_ref, pair_ref, streams_ref, xs_ref, ks_ref,
    taps_ref, rates_ref, skip_ref, short_ref, *refs
):
    tabs = refs[:4]
    gst_own_ref, gst_other_ref, gtaps_ref, sums_ref = refs[4:8]
    gg_ref, ag_ref, bx_ref, bk_ref, gs_ref, decayed_ref, decay_ref, gk_ref, acc_ref = refs[8:]
    seq_len, columns = query_ref.shape
    count = seq_len // BLOCK
    half_rows = seq_len // 2
    two_docs = flags[0] == 1
    core = flags[1]
    signal, filt = first_level(two_docs)
    decay_taps(taps_ref, rates_ref, decayed_ref, decay_ref)
    own_base = pl.multiple_of(core * half_rows, half_rows)
    other_base = pl.multiple_of((1 - core) * half_rows, half_rows)
    gg_ref[pl.ds(own_base, half_rows)] = own_ref[...].astype(F32)
    gg_ref[pl.ds(other_base, half_rows)] = other_ref[...].astype(F32)

    def load_grad(k, start, lanes):
        rows = pl.ds(k * BLOCK + start, SLAB)
        return gg_ref[rows, lanes] * query_ref[rows, lanes].astype(F32)

    blocks_in(load_grad, signal, count, columns, ag_ref)
    for leaf in range(count):
        grads = dot(forward_table(tabs, leaf), ag_ref[leaf])
        table = inverse_table(tabs, leaf)
        ks = ks_ref[leaf].astype(F32)
        bx_ref[leaf] = dot(table, complex_product(ks, grads, True))
        xs = xs_ref[leaf].astype(F32)
        bk_ref[leaf] = dot(table, complex_product(xs, grads, True))
    gs_ref[:, seq_len:] = jnp.zeros((3, PAD, columns), F32)
    acc_ref[...] = jnp.zeros(acc_ref.shape, F32)

    def store_mixed(k, start, lanes, value):
        rows = pl.ds(k * BLOCK + start, SLAB)
        gg = gg_ref[rows, lanes]
        grad_conv = gg * query_ref[rows, lanes].astype(F32)
        first = pair_ref[0, rows, lanes].astype(F32)
        second = pair_ref[1, rows, lanes].astype(F32)
        grad_mixed = grad_conv * skip_ref[:, lanes] + value
        gs_ref[0, rows, lanes] = gg * arg_ref[rows, lanes].astype(F32)
        gs_ref[1, rows, lanes] = grad_mixed * second
        gs_ref[2, rows, lanes] = grad_mixed * first
        acc_ref[13, :, lanes] += fold_rows(grad_conv * (first * second))

    blocks_out(store_mixed, signal, count, columns, bx_ref)
    gk_ref[0:PAD] = jnp.zeros((PAD, columns), F32)
    gk_ref[PAD + seq_len :] = jnp.zeros((PAD, columns), F32)

    def store_taps(k, start, lanes, value):
        pooled = three_sum(decayed_ref, k * BLOCK + start, SLAB, lanes)
        kept = jnp.where(jnp.abs(pooled) > CUT, value, 0.0)
        gk_ref[pl.ds(PAD + k * BLOCK + start, SLAB), lanes] = kept

    blocks_out(store_taps, filt, count, columns, bk_ref)

    def taps_body(step, _):
        start = pl.multiple_of(step * BLOCK, BLOCK)
        grad = three_sum(gk_ref, start, BLOCK, slice(None))
        times = (lax.broadcasted_iota(jnp.int32, (BLOCK, columns), 0) + start).astype(F32)
        gtaps_ref[pl.ds(start, BLOCK)] = (grad * decay_ref[pl.ds(start, BLOCK)]).astype(BF16)
        acc_ref[12] -= fold_rows(times * grad * decayed_ref[pl.ds(PAD + start, BLOCK)])
        return 0

    lax.fori_loop(0, count, taps_body, 0)

    def short_block(block, target_ref, target):
        start = pl.multiple_of(block * BLOCK, BLOCK)
        rows = lax.broadcasted_iota(jnp.int32, (BLOCK, columns), 0) + start
        boundary = jnp.where(two_docs, half_rows, seq_len)
        keep = [
            None,
            ((rows + 1 < boundary) | (rows >= boundary)).astype(F32),
            ((rows + 2 < boundary) | (rows >= boundary)).astype(F32),
        ]
        for s in range(3):
            stream = streams_ref[s, pl.ds(start, BLOCK)].astype(F32)
            window = gs_ref[s, pl.ds(start, BLOCK + PAD)]
            total = None
            for j in range(3):
                grad = window[j : j + BLOCK]
                if j:
                    grad = grad * keep[j]
                acc_ref[3 * j + s] += fold_rows(grad * stream)
                term = short_ref[3 * j + s : 3 * j + s + 1] * grad
                total = term if total is None else total + term
            low = total.astype(BF16)
            acc_ref[9 + s] += fold_rows(low.astype(F32))
            target_ref[s, pl.ds(target, BLOCK)] = low

    def short_body(step, _):
        target = pl.multiple_of(step * BLOCK, BLOCK)
        short_block(core * (count // 2) + step, gst_own_ref, target)
        short_block((1 - core) * (count // 2) + step, gst_other_ref, target)
        return 0

    lax.fori_loop(0, count // 2, short_body, 0)
    sums_ref[...] = jnp.sum(acc_ref[...], axis=1)


def conv_backward(flags, own, other, query, arg, pair, streams, xs, ks, taps, rates, skip, short9, tabs):
    seq_len, channels = query.shape
    count = seq_len // BLOCK
    args = (own, other, query, arg, pair, streams, xs, ks, taps, rates, skip, short9) + tabs
    spectrum = (count, 2 * BLOCK, channels)
    outs = [
        jax.ShapeDtypeStruct((3, seq_len // 2, channels), BF16),
        jax.ShapeDtypeStruct((3, seq_len // 2, channels), BF16),
        jax.ShapeDtypeStruct((seq_len, channels), BF16),
        jax.ShapeDtypeStruct((16, channels), F32),
    ]
    padded = (seq_len + 2 * PAD, channels)
    return pl.pallas_call(
        conv_back_kernel,
        grid_spec=pltpu.PrefetchScalarGridSpec(
            num_scalar_prefetch=1,
            grid=(1,),
            in_specs=[whole(item.shape) for item in args],
            out_specs=[whole(item.shape) for item in outs],
            scratch_shapes=[
                pltpu.VMEM((seq_len, channels), F32),
                pltpu.VMEM(spectrum, BF16),
                pltpu.VMEM(spectrum, F32),
                pltpu.VMEM(spectrum, F32),
                pltpu.VMEM((3, seq_len + PAD, channels), F32),
                pltpu.VMEM(padded, F32),
                pltpu.VMEM((seq_len, channels), F32),
                pltpu.VMEM(padded, F32),
                pltpu.VMEM((16, 8, channels), F32),
            ],
        ),
        out_shape=outs,
        name="conv_backward",
        cost_estimate=pl.CostEstimate(
            flops=2 * 3 * count * (2 * BLOCK) ** 2 * channels,
            bytes_accessed=seq_len * channels * 36, transcendentals=seq_len * channels,
        ),
    )(flags, *args)


def mlp_kernel(
    flags, tok_ref, own_ref, recv_ref, bias_ref, gain_ref, shift_ref, cot_ref,
    up0_ref, up1_ref, bup_ref, down0_ref, down1_ref,
    hid_ref, normed_ref, act0_ref, act1_ref, gp0_ref, gp1_ref, out_ref, gn_ref, sum_ref,
):
    step = pl.program_id(0)
    hidden_one = (
        tok_ref[...].astype(F32) + (own_ref[...].astype(F32) + recv_ref[...].astype(F32))
    ) + bias_ref[...]
    hid_ref[...] = hidden_one
    unit, _ = normalize(hidden_one)
    normed = (unit * gain_ref[...] + shift_ref[...]).astype(BF16)
    normed_ref[...] = normed
    cot = cot_ref[...]
    out_total = grad_total = None

    @pl.when(step == 0)
    def _():
        sum_ref[...] = jnp.zeros(sum_ref.shape, F32)

    for j, (up_ref, down_ref, act_ref, gp_ref) in enumerate(
        ((up0_ref, down0_ref, act0_ref, gp0_ref), (up1_ref, down1_ref, act1_ref, gp1_ref))
    ):
        pre = dot(normed, up_ref[...]) + bup_ref[j : j + 1]
        cdf = 0.5 * (1.0 + lax.erf(pre * math.sqrt(0.5)))
        slope = cdf + pre * (jnp.exp(-0.5 * pre * pre) * (1.0 / math.sqrt(2.0 * math.pi)))
        act = (pre * cdf).astype(BF16)
        act_ref[...] = act
        out_part = dot(act, down_ref[...])
        grad_pre = (dot_rhs_t(cot, down_ref[...]) * slope).astype(BF16)
        gp_ref[...] = grad_pre
        sum_ref[j] += fold_rows(grad_pre.astype(F32))
        grad_part = dot_rhs_t(grad_pre, up_ref[...])
        out_total = out_part if j == 0 else out_total + out_part
        grad_total = grad_part if j == 0 else grad_total + grad_part
    out_ref[...] = out_total.astype(BF16)
    gn_ref[...] = grad_total.astype(BF16)


def mlp(flags, chunk, chunks, tokens, own, recv, bias, gain, shift, cot, up0, up1, bup, down0, down1):
    rows, width = own.shape
    units = up0.shape[1]
    steps = rows // TILE
    half = chunks * steps

    def mine(i, flags):
        return (flags[1] * half + chunk * steps + i, 0)

    def row(i, flags):
        return (i, 0)

    wide = pl.BlockSpec((TILE, width), row)
    long = pl.BlockSpec((TILE, units), row)
    return pl.pallas_call(
        mlp_kernel,
        grid_spec=pltpu.PrefetchScalarGridSpec(
            num_scalar_prefetch=1,
            grid=(steps,),
            in_specs=[
                pl.BlockSpec((TILE, width), mine), wide, wide,
                whole((1, width)), whole((1, width)), whole((1, width)),
                pl.BlockSpec((TILE, width), mine),
                whole(up0.shape), whole(up0.shape), whole(bup.shape),
                whole(down0.shape), whole(down0.shape),
            ],
            out_specs=[wide, wide, long, long, long, long, wide, wide, whole((2, 8, units))],
        ),
        out_shape=[
            jax.ShapeDtypeStruct((rows, width), F32),
            jax.ShapeDtypeStruct((rows, width), BF16),
            jax.ShapeDtypeStruct((rows, units), BF16),
            jax.ShapeDtypeStruct((rows, units), BF16),
            jax.ShapeDtypeStruct((rows, units), BF16),
            jax.ShapeDtypeStruct((rows, units), BF16),
            jax.ShapeDtypeStruct((rows, width), BF16),
            jax.ShapeDtypeStruct((rows, width), BF16),
            jax.ShapeDtypeStruct((2, 8, units), F32),
        ],
        name="mlp",
        cost_estimate=pl.CostEstimate(
            flops=2 * 8 * rows * width * units,
            bytes_accessed=rows * (width * 16 + units * 8) + 8 * width * units,
            transcendentals=2 * rows * units,
        ),
    )(flags, tokens, own, recv, bias, gain, shift, cot, up0, up1, bup, down0, down1)


def mlp_back_kernel(
    flags, hid_ref, own_ref, recv_ref, cot_ref, gain_ref, po0_ref, po1_ref,
    gh_ref, ga_ref, gg0_ref, gg1_ref, sum_ref,
):
    unit, rate = normalize(hid_ref[...])
    grad = own_ref[...].astype(F32) + recv_ref[...].astype(F32)
    grad_hidden = cot_ref[...].astype(F32) + norm_back(grad, unit, rate, gain_ref[...])
    gh_ref[...] = grad_hidden
    low = grad_hidden.astype(BF16)
    ga_ref[...] = low
    gg0_ref[...] = dot_rhs_t(low, po0_ref[...]).astype(BF16)
    gg1_ref[...] = dot_rhs_t(low, po1_ref[...]).astype(BF16)

    @pl.when(pl.program_id(0) == 0)
    def _():
        sum_ref[...] = jnp.zeros(sum_ref.shape, F32)

    sum_ref[0] += fold_rows(grad * unit)
    sum_ref[1] += fold_rows(grad)
    sum_ref[2] += fold_rows(grad_hidden)
    sum_ref[3] += fold_rows(cot_ref[...].astype(F32))


def mlp_back(flags, chunk, chunks, hid, own, recv, cot, gain, po0, po1):
    rows, width = own.shape
    channels = po0.shape[0]
    steps = rows // TILE
    half = chunks * steps

    def mine(i, flags):
        return (flags[1] * half + chunk * steps + i, 0)

    def row(i, flags):
        return (i, 0)

    wide = pl.BlockSpec((TILE, width), row)
    thin = pl.BlockSpec((TILE, channels), row)
    return pl.pallas_call(
        mlp_back_kernel,
        grid_spec=pltpu.PrefetchScalarGridSpec(
            num_scalar_prefetch=1,
            grid=(steps,),
            in_specs=[
                wide, wide, wide, pl.BlockSpec((TILE, width), mine),
                whole((1, width)), whole(po0.shape), whole(po0.shape),
            ],
            out_specs=[wide, wide, thin, thin, whole((4, 8, width))],
        ),
        out_shape=[
            jax.ShapeDtypeStruct((rows, width), F32),
            jax.ShapeDtypeStruct((rows, width), BF16),
            jax.ShapeDtypeStruct((rows, channels), BF16),
            jax.ShapeDtypeStruct((rows, channels), BF16),
            jax.ShapeDtypeStruct((4, 8, width), F32),
        ],
        name="mlp_back",
        cost_estimate=pl.CostEstimate(
            flops=4 * rows * width * channels, bytes_accessed=rows * width * 16, transcendentals=0
        ),
    )(flags, hid, own, recv, cot, gain, po0, po1)


def streams_back_kernel(flags, g0_ref, g1_ref, w0_ref, w1_ref, tok_ref, gn_ref, sum_ref):
    total = None
    for g_ref, w_ref in ((g0_ref, w0_ref), (g1_ref, w1_ref)):
        for s in range(3):
            term = dot_rhs_t(g_ref[s], w_ref[s])
            total = term if total is None else total + term
    low = total.astype(BF16)
    gn_ref[...] = low
    part = low.astype(F32)
    unit, _ = normalize(tok_ref[...].astype(F32))

    @pl.when(pl.program_id(0) == 0)
    def _():
        sum_ref[...] = jnp.zeros(sum_ref.shape, F32)

    sum_ref[0] += fold_rows(part * unit)
    sum_ref[1] += fold_rows(part)


def streams_back(flags, chunk, chunks, g0, g1, w0, w1, tokens):
    width = tokens.shape[1]
    channels = g0.shape[2]
    rows = g0.shape[1] // chunks
    steps = rows // TILE
    half = chunks * steps
    part = pl.BlockSpec((3, TILE, channels), lambda i, f: (0, chunk * steps + i, 0))
    return pl.pallas_call(
        streams_back_kernel,
        grid_spec=pltpu.PrefetchScalarGridSpec(
            num_scalar_prefetch=1,
            grid=(steps,),
            in_specs=[
                part, part, whole(w0.shape), whole(w0.shape),
                pl.BlockSpec((TILE, width), lambda i, f: (f[1] * half + chunk * steps + i, 0)),
            ],
            out_specs=[pl.BlockSpec((TILE, width), lambda i, f: (i, 0)), whole((2, 8, width))],
        ),
        out_shape=[
            jax.ShapeDtypeStruct((rows, width), BF16),
            jax.ShapeDtypeStruct((2, 8, width), F32),
        ],
        name="streams_back",
        cost_estimate=pl.CostEstimate(
            flops=2 * rows * width * 6 * channels, bytes_accessed=rows * width * 8, transcendentals=0
        ),
    )(flags, g0, g1, w0, w1, tokens)


def input_back_kernel(flags, tok_ref, own_ref, recv_ref, gain_ref, gh_ref, out_ref):
    unit, rate = normalize(tok_ref[...].astype(F32))
    grad = own_ref[...].astype(F32) + recv_ref[...].astype(F32)
    out_ref[...] = gh_ref[...] + norm_back(grad, unit, rate, gain_ref[...])


def input_back(flags, chunk, chunks, tokens, own, recv, gain, gh):
    rows, width = own.shape
    steps = rows // TILE
    half = chunks * steps
    wide = pl.BlockSpec((TILE, width), lambda i, f: (i, 0))
    return pl.pallas_call(
        input_back_kernel,
        grid_spec=pltpu.PrefetchScalarGridSpec(
            num_scalar_prefetch=1,
            grid=(steps,),
            in_specs=[
                pl.BlockSpec((TILE, width), lambda i, f: (f[1] * half + chunk * steps + i, 0)),
                wide, wide, whole((1, width)), wide,
            ],
            out_specs=wide,
        ),
        out_shape=jax.ShapeDtypeStruct((rows, width), F32),
        name="input_back",
        cost_estimate=pl.CostEstimate(
            flops=rows * width * 20, bytes_accessed=rows * width * 14, transcendentals=0
        ),
    )(flags, tokens, own, recv, gain, gh)


def swap_core(value, size):
    return lax.ppermute(value, "mp", [(i, i ^ 1) for i in range(size)])


def across_x(value, size):
    chips = size // 2
    if chips == 1:
        return value, jnp.zeros_like(value)
    if chips == 2:
        return value, lax.ppermute(value, "mp", [(i, i ^ 2) for i in range(size)])
    terms = [value.astype(F32)]
    for shift in range(1, chips):
        pairs = [(i, (i + 2 * shift) % size) for i in range(size)]
        terms.append(lax.ppermute(value, "mp", pairs).astype(F32))
    here = lax.axis_index("mp") // 2
    stacked = jnp.stack(terms)
    total = 0.0
    for chip in range(chips):
        total = total + lax.dynamic_index_in_dim(stacked, (here - chip) % chips, 0, keepdims=False)
    high = total.astype(BF16)
    return high, (total - high.astype(F32)).astype(BF16)


def dp_pairs(size, stride):
    return [(i, i ^ stride) for i in range(size)]


def as_bits(value, size):
    bits = size.bit_length() - 1
    return value.reshape((2,) * bits + (value.shape[0] // size,) + value.shape[1:]), bits


def dp_scatter(value, size, order):
    here = lax.axis_index("dp")
    value, bits = as_bits(value, size)
    for bit in order:
        axis = bits - 1 - bit
        side = (here >> bit) & 1
        send = lax.dynamic_slice_in_dim(value, 1 - side, 1, axis).astype(BF16)
        keep = lax.dynamic_slice_in_dim(value, side, 1, axis)
        value = keep + lax.ppermute(send, "dp", dp_pairs(size, 1 << bit)).astype(F32)
    return value.reshape(value.shape[bits:])


def dp_gather(value, size, order):
    here = lax.axis_index("dp")
    bits = size.bit_length() - 1
    rows = value.shape[0]
    value = value.reshape((1,) * bits + value.shape)
    for bit in order:
        axis = bits - 1 - bit
        other = lax.ppermute(value, "dp", dp_pairs(size, 1 << bit))
        side = (here >> bit) & 1
        value = jnp.where(
            side == 1,
            jnp.concatenate([other, value], axis),
            jnp.concatenate([value, other], axis),
        )
    return value.reshape((size * rows,) + value.shape[bits + 1 :])


def dp_total(value, size, first):
    bits = size.bit_length() - 1
    order = [first] + [bit for bit in range(bits) if bit != first]
    part = dp_scatter(value, size, order).astype(BF16)
    return dp_gather(part, size, order[::-1])


def dp_exchange_total(value, size):
    for bit in range(size.bit_length() - 1):
        value = value + lax.ppermute(value, "dp", dp_pairs(size, 1 << bit))
    return value


def per_device(
    dp, mp,
    tokens, lengths, mix_gain, mix_shift, proj_in, bias_in, short_taps, long_taps, decay_rates,
    skip_gain, proj_out, bias_out, mlp_gain, mlp_shift, proj_up, bias_up, proj_down, bias_down,
    cotangent,
):
    seq_len, width = tokens.shape
    channels = proj_in.shape[2]
    units = proj_up.shape[1]
    half = seq_len // 2
    rows = half // CHUNKS
    core = (lax.axis_index("mp") % 2).astype(jnp.int32)
    two_docs = (lengths[0, 0] < seq_len).astype(jnp.int32)
    flags = jnp.stack([two_docs, core])
    row = lambda vec: vec.reshape(1, -1)
    swap = lambda value: swap_core(value, mp)
    tabs = tables(seq_len)

    order = list(range(dp.bit_length() - 1))[::-1]
    taps = dp_gather(long_taps, dp, order)
    w3 = jnp.transpose(proj_in, (1, 0, 2))
    w3_other = swap(w3)
    po_other = swap(proj_out)
    up_other = swap(proj_up)
    down_other = swap(proj_down)
    bup = jnp.stack([bias_up, swap(bias_up)])

    short9 = short_taps.reshape(9, channels)
    normed, streams, query, pair, mixed = mixer_in(
        flags, tokens, row(mix_gain), row(mix_shift), w3, bias_in, short9
    )
    gated, arg, xs, ks = conv_forward(
        flags, mixed, query, taps, row(decay_rates), row(skip_gain), tabs
    )
    gated_own = gated[:half]
    gated_other = swap(gated[half:])

    outs, grads, states = [], [], []
    for c in range(CHUNKS):
        part = slice(c * rows, (c + 1) * rows)
        attn = (dot(gated_own[part], proj_out) + dot(gated_other[part], po_other)).astype(BF16)
        own, recv = across_x(attn, mp)
        hid, normed_two, act0, act1, gp0, gp1, down, gnorm, bsum = mlp(
            flags, c, CHUNKS, tokens, own, recv, row(bias_out), row(mlp_gain), row(mlp_shift),
            cotangent, proj_up, up_other, bup, proj_down, down_other,
        )
        grads.append(across_x(gnorm, mp))
        outs.append(down)
        states.append((hid, normed_two, act0, act1, gp0, gp1, bsum))
    join = lambda k: jnp.concatenate([state[k] for state in states], axis=0)
    hid_all = [state[0] for state in states]

    cot_own = lax.dynamic_slice_in_dim(cotangent, core * half, half, 0)
    normed_two, act0, act1, gp0, gp1 = (join(k) for k in range(1, 6))
    g_down = dot_lhs_t(act0, cot_own) + swap(dot_lhs_t(act1, cot_own).astype(BF16)).astype(F32)
    g_up = dot_lhs_t(normed_two, gp0) + swap(dot_lhs_t(normed_two, gp1).astype(BF16)).astype(F32)
    bup_sum = jnp.sum(sum(state[6] for state in states), axis=1)
    g_bias_up = bup_sum[0] + swap(bup_sum[1])

    gh, ga, gg0, gg1, sums = [], [], [], [], 0.0
    for c in range(CHUNKS):
        own, recv = grads[c]
        part = mlp_back(
            flags, c, CHUNKS, hid_all[c], own, recv, cotangent, row(mlp_gain), proj_out, po_other
        )
        gh.append(part[0])
        ga.append(part[1])
        gg0.append(part[2])
        gg1.append(part[3])
        sums = sums + part[4]
    sums = jnp.sum(sums, axis=1)
    ga = jnp.concatenate(ga, axis=0)
    gg_own = jnp.concatenate(gg0, axis=0)
    gg_other = swap(jnp.concatenate(gg1, axis=0))
    g_po = dot_lhs_t(gated_own, ga) + swap(dot_lhs_t(gated_other, ga).astype(BF16)).astype(F32)

    gst_own, gst_send, g_taps, conv_sums = conv_backward(
        flags, gg_own, gg_other, query, arg, pair, streams, xs, ks, taps, row(decay_rates),
        row(skip_gain), short9, tabs,
    )
    gst_recv = swap(gst_send)
    g_in = jnp.stack(
        [
            dot_lhs_t(normed[:half], gst_own[s]) + dot_lhs_t(normed[half:], gst_send[s])
            for s in range(3)
        ]
    )

    finals, norm_sums = [], 0.0
    for c in range(CHUNKS):
        gnorm, part = streams_back(flags, c, CHUNKS, gst_own, gst_recv, w3, w3_other, tokens)
        own, recv = across_x(gnorm, mp)
        finals.append(input_back(flags, c, CHUNKS, tokens, own, recv, row(mix_gain), gh[c]))
        norm_sums = norm_sums + part
    norm_sums = jnp.sum(norm_sums, axis=1)

    def both_rows(mine):
        other = swap(mine)
        return jnp.where(
            core == 0, jnp.concatenate([mine, other], 0), jnp.concatenate([other, mine], 0)
        )

    input_grad = both_rows(jnp.concatenate(finals, axis=0))
    out_rows = []
    for c in range(CHUNKS):
        own, recv = across_x(outs[c], mp)
        out_rows.append(
            (hid_all[c] + (own.astype(F32) + recv.astype(F32)) + row(bias_down)).astype(BF16)
        )
    output = both_rows(jnp.concatenate(out_rows, axis=0))

    two_x = norm_sums
    chips = mp // 2
    total_x = two_x
    for shift in range(1, chips):
        total_x = total_x + lax.ppermute(
            two_x, "mp", [(i, (i + 2 * shift) % mp) for i in range(mp)]
        )
    shared = jnp.concatenate([total_x, sums], axis=0)
    shared = shared + swap(shared)
    small = jnp.concatenate([shared.reshape(-1), conv_sums[:14].reshape(-1), g_bias_up])
    small = dp_exchange_total(small, dp)
    shared = small[: 6 * width].reshape(6, width)
    conv_sums = small[6 * width : 6 * width + 14 * channels].reshape(14, channels)
    g_bias_up = small[6 * width + 14 * channels :]

    g_down = dp_total(g_down, dp, 0).astype(F32)
    g_up = dp_total(g_up, dp, 1).astype(F32)
    g_po = dp_total(g_po, dp, 0).astype(F32)
    g_in = dp_total(g_in.reshape(3 * width, channels), dp, 1)
    g_in = jnp.transpose(g_in.reshape(3, width, channels), (1, 0, 2)).astype(F32)
    g_taps = dp_scatter(g_taps.astype(F32), dp, list(range(dp.bit_length() - 1)))

    return (
        output,
        input_grad,
        shared[0],
        shared[1],
        g_in,
        conv_sums[9:12],
        conv_sums[:9].reshape(3, 3, channels),
        g_taps,
        conv_sums[12],
        conv_sums[13],
        g_po,
        shared[4],
        shared[2],
        shared[3],
        g_up,
        g_bias_up,
        g_down,
        shared[5],
    )


def solution(mesh):
    in_specs = (
        P("dp", None), P("dp", None), P(), P(), P(None, None, "mp"), P(None, "mp"),
        P(None, None, "mp"), P("dp", "mp"), P("mp"), P("mp"), P("mp", None), P(), P(), P(),
        P(None, "mp"), P("mp"), P("mp", None), P(), P("dp", None),
    )
    out_specs = (
        P("dp", None), P("dp", None), P(), P(), P(None, None, "mp"), P(None, "mp"),
        P(None, None, "mp"), P("dp", "mp"), P("mp"), P("mp"), P("mp", None), P(), P(), P(),
        P(None, "mp"), P("mp"), P("mp", None), P(),
    )
    body = partial(per_device, mesh.shape["dp"], mesh.shape["mp"])
    return jax.shard_map(
        body, mesh=mesh, in_specs=in_specs, out_specs=out_specs, check_vma=False
    )
```

```python
from functools import partial
import math

import jax
import jax.numpy as jnp
import numpy as np
from jax import lax
from jax.experimental import pallas as pl
from jax.experimental.pallas import tpu as pltpu
from jax.sharding import PartitionSpec as P

F32 = jnp.float32
BF16 = jnp.bfloat16
EPS = 1e-05
CUT = 0.003
BLOCK = 128
SLAB = 16
TILE = 256
CHUNKS = 2
PAD = 8


def dot(lhs, rhs):
    return jnp.dot(lhs, rhs, preferred_element_type=F32)


def dot_rhs_t(lhs, rhs):
    return lax.dot_general(lhs, rhs, (((1,), (1,)), ((), ())), preferred_element_type=F32)


def dot_lhs_t(lhs, rhs):
    return lax.dot_general(lhs, rhs, (((0,), (0,)), ((), ())), preferred_element_type=F32)


def normalize(values):
    centered = values - jnp.mean(values, axis=-1, keepdims=True)
    rate = lax.rsqrt(jnp.mean(centered * centered, axis=-1, keepdims=True) + EPS)
    return centered * rate, rate


def norm_back(grad, unit, rate, gain):
    back = grad * gain
    mean_back = jnp.mean(back, axis=-1, keepdims=True)
    mean_unit = jnp.mean(back * unit, axis=-1, keepdims=True)
    return rate * (back - mean_back - unit * mean_unit)


def cost(microseconds=0):
    return pl.CostEstimate(
        flops=int(microseconds * 1e9), bytes_accessed=int(microseconds * 3.6e6), transcendentals=0
    )


def lane_parts(columns):
    return [(low, min(low + 128, columns)) for low in range(0, columns, 128)]


def whole(shape):
    zeros = (0,) * len(shape)
    return pl.BlockSpec(shape, lambda *_: zeros)


def limit(mebibytes):
    return pltpu.CompilerParams(vmem_limit_bytes=mebibytes << 20)


SCALARS = pl.BlockSpec(memory_space=pltpu.SMEM)
RESIDENT = pl.BlockSpec(memory_space=pltpu.VMEM)
ANYWHERE = pl.BlockSpec(memory_space=pl.ANY)


def fold_rows(values):
    rows, columns = values.shape
    return jnp.sum(values.reshape(rows // 8, 8, columns), axis=0)


def leaf_angles(count, angle):
    if count == 1:
        return [angle]
    return leaf_angles(count // 2, angle / 2) + leaf_angles(count // 2, angle / 2 + math.pi)


def split_tree(real, imag, angle):
    count = len(real)
    if count == 1:
        return [(real[0], imag[0])]
    half = count // 2
    cos, sin = math.cos(angle / 2), math.sin(angle / 2)
    plus, minus = ([], []), ([], [])
    for k in range(half):
        turned_re = cos * real[k + half] - sin * imag[k + half]
        turned_im = sin * real[k + half] + cos * imag[k + half]
        plus[0].append(real[k] + turned_re)
        plus[1].append(imag[k] + turned_im)
        minus[0].append(real[k] - turned_re)
        minus[1].append(imag[k] - turned_im)
    return split_tree(*plus, angle / 2) + split_tree(*minus, angle / 2 + math.pi)


def join_tree(leaves, angle):
    count = len(leaves)
    if count == 1:
        return [leaves[0][0]], [leaves[0][1]]
    half = count // 2
    cos, sin = math.cos(angle / 2), math.sin(angle / 2)
    plus = join_tree(leaves[:half], angle / 2)
    minus = join_tree(leaves[half:], angle / 2 + math.pi)
    low_re, low_im, high_re, high_im = [], [], [], []
    for k in range(half):
        diff_re = plus[0][k] - minus[0][k]
        diff_im = plus[1][k] - minus[1][k]
        low_re.append(plus[0][k] + minus[0][k])
        low_im.append(plus[1][k] + minus[1][k])
        high_re.append(cos * diff_re + sin * diff_im)
        high_im.append(cos * diff_im - sin * diff_re)
    return low_re + high_re, low_im + high_im


def tables(seq_len):
    count = seq_len // BLOCK
    angles = np.array(leaf_angles(count, math.pi / 2))
    index = np.arange(BLOCK)
    base = 2 * np.pi * np.outer(index, index) / BLOCK
    turn = np.outer(angles, index) / BLOCK
    rows = np.concatenate([np.cos(turn), np.sin(turn)], 0)
    columns = rows.T / seq_len
    return tuple(
        jnp.asarray(item.astype(np.float32)) for item in (np.cos(base), np.sin(base), rows, columns)
    )


def forward_table(tabs, leaf):
    cos_b, sin_b, rows, _ = tabs
    count = rows.shape[0] // 2
    cos_t = rows[leaf : leaf + 1, :]
    sin_t = rows[count + leaf : count + leaf + 1, :]
    cos = cos_b[...] * cos_t - sin_b[...] * sin_t
    sin = sin_b[...] * cos_t + cos_b[...] * sin_t
    top = jnp.concatenate([cos, -sin], axis=1)
    bottom = jnp.concatenate([sin, cos], axis=1)
    return jnp.concatenate([top, bottom], axis=0).astype(BF16)


def inverse_table(tabs, leaf):
    cos_b, sin_b, _, columns = tabs
    count = columns.shape[1] // 2
    cos_t = columns[:, leaf : leaf + 1]
    sin_t = columns[:, count + leaf : count + leaf + 1]
    cos = cos_b[...] * cos_t - sin_b[...] * sin_t
    sin = sin_b[...] * cos_t + cos_b[...] * sin_t
    top = jnp.concatenate([cos, sin], axis=1)
    bottom = jnp.concatenate([-sin, cos], axis=1)
    return jnp.concatenate([top, bottom], axis=0).astype(BF16)


def first_level(two_docs):
    one = jnp.where(two_docs, 0.0, 1.0).astype(F32)
    root = math.sqrt(0.5)
    signal = (root * one, root * one + (1.0 - one), 1.0 - 2.0 * one)
    filt = (root * one, root * one, 1.0 - 2.0 * one)
    return signal, filt


def blocks_in(load, level, count, columns, out_ref):
    cos, sin, sign = level
    half = count // 2

    def body(step, _):
        start = pl.multiple_of(step * SLAB, SLAB)
        for part in lane_parts(columns):
            lanes = slice(*part)
            items = [load(k, start, lanes) for k in range(count)]
            for branch in range(2):
                angle = math.pi / 4 + branch * math.pi
                c = cos * sign if branch else cos
                s = sin * sign if branch else sin
                real = [items[k] + c * items[k + half] for k in range(half)]
                imag = [s * items[k + half] for k in range(half)]
                leaves = split_tree(real, imag, angle)
                for leaf, (re, im) in enumerate(leaves):
                    where = branch * half + leaf
                    out_ref[where, pl.ds(start, SLAB), lanes] = re.astype(BF16)
                    out_ref[where, pl.ds(BLOCK + start, SLAB), lanes] = im.astype(BF16)
        return 0

    lax.fori_loop(0, BLOCK // SLAB, body, 0)


def blocks_out(store, level, count, columns, in_ref):
    cos, sin, sign = level
    half = count // 2

    def body(step, _):
        start = pl.multiple_of(step * SLAB, SLAB)
        for part in lane_parts(columns):
            lanes = slice(*part)
            joined = []
            for branch in range(2):
                leaves = []
                for leaf in range(half):
                    where = branch * half + leaf
                    leaves.append(
                        (
                            in_ref[where, pl.ds(start, SLAB), lanes],
                            in_ref[where, pl.ds(BLOCK + start, SLAB), lanes],
                        )
                    )
                joined.append(join_tree(leaves, math.pi / 4 + branch * math.pi))
            (plus_re, plus_im), (minus_re, minus_im) = joined
            for k in range(half):
                store(k, start, lanes, plus_re[k] + minus_re[k])
                high = cos * (plus_re[k] + sign * minus_re[k]) + sin * (
                    plus_im[k] + sign * minus_im[k]
                )
                store(k + half, start, lanes, high)
        return 0

    lax.fori_loop(0, BLOCK // SLAB, body, 0)


def complex_product(left, right, conjugate):
    l_re, l_im = left[:BLOCK], left[BLOCK:]
    r_re, r_im = right[:BLOCK], right[BLOCK:]
    if conjugate:
        real, imag = l_re * r_re + l_im * r_im, l_re * r_im - l_im * r_re
    else:
        real, imag = l_re * r_re - l_im * r_im, l_re * r_im + l_im * r_re
    return jnp.concatenate([real, imag], axis=0).astype(BF16)


def decay_taps(taps_ref, rates_ref, decayed_ref, decay_ref):
    shards, lines, width = taps_ref.shape
    columns = decayed_ref.shape[1]
    seq_len = shards * lines * width // columns
    rates = rates_ref[...].reshape(1, columns)
    pad = jnp.zeros((PAD, columns), F32)
    decayed_ref[0:PAD] = pad
    decayed_ref[PAD + seq_len :] = pad

    def body(shard, _):
        for group in range(width // columns):
            start = pl.multiple_of((shard * (width // columns) + group) * lines, lines)
            times = (lax.broadcasted_iota(jnp.int32, (lines, columns), 0) + start).astype(F32)
            decay = jnp.exp(-rates * times)
            taps = taps_ref[shard, :, group * columns : (group + 1) * columns].astype(F32)
            decayed_ref[pl.ds(PAD + start, lines)] = taps * decay
            if decay_ref is not None:
                decay_ref[pl.ds(start, lines)] = decay
        return 0

    lax.fori_loop(0, shards, body, 0)


def three_sum(ref, row, size, lanes):
    window = ref[pl.ds(pl.multiple_of(row, 8), size + 2 * PAD), lanes]
    total = window[PAD - 1 : PAD - 1 + size] + window[PAD : PAD + size]
    return (total + window[PAD + 1 : PAD + 1 + size]) / 3.0


def mixer_in_kernel(
    flags, tok_ref, gain_ref, shift_ref, w_ref, b_ref, taps_ref, *refs
):
    tabs = refs[:4]
    normed_ref, streams_ref, pair_ref, query_ref, mixed_out, xs_out = refs[4:10]
    halo_ref, mixed_ref, ax_ref, xs_ref, sems = refs[10:]
    step = pl.program_id(0)
    tiles = pl.num_programs(0)
    rows = tok_ref.shape[0]
    unit, _ = normalize(tok_ref[...].astype(F32))
    normed = (unit * gain_ref[...] + shift_ref[...]).astype(BF16)
    normed_ref[...] = normed
    fresh = (step == 0) | ((flags[0] == 1) & (step * 2 == tiles))

    @pl.when(fresh)
    def _():
        halo_ref[:, 0:PAD] = jnp.zeros((3, PAD, halo_ref.shape[2]), F32)

    @pl.when(jnp.logical_not(fresh))
    def _():
        halo_ref[:, 0:PAD] = halo_ref[:, rows : rows + PAD]

    short = []
    for s in range(3):
        stream = dot_rhs_t(normed, w_ref[s]) + b_ref[s : s + 1]
        halo_ref[s, PAD:] = stream
        streams_ref[s] = stream.astype(BF16)
        short.append(
            taps_ref[0, s : s + 1] * stream
            + taps_ref[1, s : s + 1] * halo_ref[s, PAD - 1 : PAD - 1 + rows]
            + taps_ref[2, s : s + 1] * halo_ref[s, PAD - 2 : PAD - 2 + rows]
        )
    here = pl.ds(pl.multiple_of(step * rows, rows), rows)
    query_ref[...] = short[0].astype(BF16)
    pair_ref[0] = short[1].astype(BF16)
    pair_ref[1] = short[2].astype(BF16)
    product = short[1] * short[2]
    mixed_ref[here] = product
    mixed_out[...] = product

    @pl.when(step == tiles - 1)
    def _():
        seq_len, columns = mixed_ref.shape
        count = seq_len // BLOCK
        signal, _ = first_level(flags[0] == 1)

        def load(k, start, lanes):
            return mixed_ref[pl.ds(k * BLOCK + start, SLAB), lanes]

        blocks_in(load, signal, count, columns, ax_ref)
        copies = []
        for leaf in range(count):
            xs_ref[leaf] = dot(forward_table(tabs, leaf), ax_ref[leaf]).astype(BF16)
            if leaf % 4 == 3:
                part = pl.ds(leaf - 3, 4)
                copies.append(
                    pltpu.make_async_copy(xs_ref.at[part], xs_out.at[part], sems.at[leaf // 4])
                )
                copies[-1].start()
        for copy in copies:
            copy.wait()


def mixer_in(flags, tokens, gain, shift, w3, bias3, taps3, tabs):
    seq_len, width = tokens.shape
    channels = w3.shape[1]
    tiles = seq_len // TILE
    spectrum = (seq_len // BLOCK, 2 * BLOCK, channels)

    def rot(i, flags):
        return (lax.rem(i + flags[1] * (tiles // 2), tiles), 0)

    fixed = (gain, shift, w3, bias3, taps3) + tabs
    return pl.pallas_call(
        mixer_in_kernel,
        grid_spec=pltpu.PrefetchScalarGridSpec(
            num_scalar_prefetch=1,
            grid=(tiles,),
            in_specs=[pl.BlockSpec((TILE, width), lambda i, f: (i, 0))]
            + [whole(item.shape) for item in fixed],
            out_specs=[
                pl.BlockSpec((TILE, width), rot),
                pl.BlockSpec((3, TILE, channels), lambda i, f: (0, i, 0)),
                pl.BlockSpec((2, TILE, channels), lambda i, f: (0, i, 0)),
                pl.BlockSpec((TILE, channels), lambda i, f: (i, 0)),
                pl.BlockSpec((TILE, channels), lambda i, f: (i, 0)),
                ANYWHERE,
            ],
            scratch_shapes=[
                pltpu.VMEM((3, TILE + PAD, channels), F32),
                pltpu.VMEM((seq_len, channels), F32),
                pltpu.VMEM(spectrum, BF16),
                pltpu.VMEM(spectrum, BF16),
                pltpu.SemaphoreType.DMA((spectrum[0] // 4,)),
            ],
        ),
        out_shape=[
            jax.ShapeDtypeStruct((seq_len, width), BF16),
            jax.ShapeDtypeStruct((3, seq_len, channels), BF16),
            jax.ShapeDtypeStruct((2, seq_len, channels), BF16),
            jax.ShapeDtypeStruct((seq_len, channels), BF16),
            jax.ShapeDtypeStruct((seq_len, channels), F32),
            jax.ShapeDtypeStruct(spectrum, BF16),
        ],
        name="mixer_in",
        cost_estimate=cost(),
    )(flags, tokens, *fixed)


def conv_kernel(flags, mixed_in, query_in, xs_in, taps_ref, rates_ref, skip_ref, *refs):
    tabs = refs[:4]
    own_ref, other_ref, arg_out, ks_out = refs[4:8]
    mixed_ref, query_ref, xs_ref, arg_ref, ks_ref, decayed_ref, ak_ref, bb_ref, gated_ref, sems = (
        refs[8:]
    )
    seq_len, columns = mixed_in.shape
    count = seq_len // BLOCK
    get_xs = pltpu.make_async_copy(xs_in, xs_ref, sems.at[0])
    get_mixed = pltpu.make_async_copy(mixed_in, mixed_ref, sems.at[1])
    get_query = pltpu.make_async_copy(query_in, query_ref, sems.at[2])
    keep_ks = pltpu.make_async_copy(ks_ref, ks_out, sems.at[3])
    keep_arg = pltpu.make_async_copy(arg_ref, arg_out, sems.at[4])
    for copy in (get_xs, get_mixed, get_query):
        copy.start()
    signal, filt = first_level(flags[0] == 1)
    decay_taps(taps_ref, rates_ref, decayed_ref, None)
    skip = skip_ref[...].reshape(1, columns)

    def load_taps(k, start, lanes):
        pooled = three_sum(decayed_ref, k * BLOCK + start, SLAB, lanes)
        return pooled - jnp.minimum(jnp.maximum(pooled, -CUT), CUT)

    blocks_in(load_taps, filt, count, columns, ak_ref)
    get_xs.wait()
    for leaf in range(count):
        ks = dot(forward_table(tabs, leaf), ak_ref[leaf])
        ks_ref[leaf] = ks.astype(BF16)
        product = complex_product(ks, xs_ref[leaf].astype(F32), False)
        bb_ref[leaf] = dot(inverse_table(tabs, leaf), product)
    keep_ks.start()
    get_mixed.wait()
    get_query.wait()

    def store(k, start, lanes, value):
        rows = pl.ds(k * BLOCK + start, SLAB)
        arg = value + skip[:, lanes] * mixed_ref[rows, lanes]
        arg_ref[rows, lanes] = arg.astype(BF16)
        gated_ref[rows, lanes] = (query_ref[rows, lanes].astype(F32) * arg).astype(BF16)

    blocks_out(store, signal, count, columns, bb_ref)
    keep_arg.start()
    size = seq_len // 2 // CHUNKS
    for c in range(CHUNKS):
        lanes = slice(c * columns, (c + 1) * columns)
        for target_ref, core in ((own_ref, flags[1]), (other_ref, 1 - flags[1])):
            start = pl.multiple_of((core * CHUNKS + c) * size, size)
            target_ref[:, lanes] = gated_ref[pl.ds(start, size)]
    for copy in (keep_ks, keep_arg):
        copy.wait()


def conv_forward(flags, mixed, query, xs, taps, rates, skip, tabs):
    seq_len, channels = mixed.shape
    count = seq_len // BLOCK
    args = (mixed, query, xs, taps, rates, skip) + tabs
    spectrum = (count, 2 * BLOCK, channels)
    packed = (seq_len // 2 // CHUNKS, CHUNKS * channels)
    outs = [
        jax.ShapeDtypeStruct(shape, BF16)
        for shape in (
            packed, packed, (seq_len, channels), spectrum
        )
    ]
    return pl.pallas_call(
        conv_kernel,
        grid_spec=pltpu.PrefetchScalarGridSpec(
            num_scalar_prefetch=1,
            grid=(1,),
            in_specs=[ANYWHERE] * 3 + [whole(item.shape) for item in args[3:]],
            out_specs=[whole(packed)] * 2 + [ANYWHERE] * 2,
            scratch_shapes=[
                pltpu.VMEM((seq_len, channels), F32),
                pltpu.VMEM((seq_len, channels), BF16),
                pltpu.VMEM(spectrum, BF16),
                pltpu.VMEM((seq_len, channels), BF16),
                pltpu.VMEM(spectrum, BF16),
                pltpu.VMEM((seq_len + 2 * PAD, channels), F32),
                pltpu.VMEM(spectrum, BF16),
                pltpu.VMEM(spectrum, F32),
                pltpu.VMEM((seq_len, channels), BF16),
                pltpu.SemaphoreType.DMA((5,)),
            ],
        ),
        out_shape=outs,
        name="conv_forward",
        cost_estimate=cost(),
    )(flags, *args)


def conv_back_kernel(
    flags, query_in, ks_in, xs_in, arg_in, pair_in, streams_in,
    taps_ref, rates_ref, skip_ref, short_ref, *refs
):
    query_ref, ks_ref, xs_ref, arg_ref, pair_ref, streams_ref, sems = refs[-7:]
    refs = refs[:-7]
    copies = [
        pltpu.make_async_copy(source, target, sems.at[k])
        for k, (source, target) in enumerate(
            (
                (query_in, query_ref), (ks_in, ks_ref), (xs_in, xs_ref), (arg_in, arg_ref),
                (pair_in, pair_ref), (streams_in, streams_ref),
            )
        )
    ]
    for copy in copies:
        copy.start()
    own_refs, other_refs, refs = refs[:CHUNKS], refs[CHUNKS : 2 * CHUNKS], refs[2 * CHUNKS :]
    tabs = refs[:4]
    gst_own_ref, gst_other_ref, packed_ref, gtaps_ref, sums_ref = refs[4:9]
    gg_ref, ag_ref, bx_ref, bk_ref, gs_ref, decayed_ref, decay_ref, gk_ref, acc_ref = refs[9:]
    seq_len, columns = query_ref.shape
    count = seq_len // BLOCK
    half_rows = seq_len // 2
    two_docs = flags[0] == 1
    core = flags[1]
    signal, filt = first_level(two_docs)
    skip = skip_ref[...].reshape(1, columns)
    decay_taps(taps_ref, rates_ref, decayed_ref, decay_ref)
    own_base = pl.multiple_of(core * half_rows, half_rows)
    other_base = pl.multiple_of((1 - core) * half_rows, half_rows)
    size = half_rows // CHUNKS
    for base, items in ((own_base, own_refs), (other_base, other_refs)):
        for c in range(CHUNKS):
            start = pl.multiple_of(base + c * size, size)
            gg_ref[pl.ds(start, size)] = items[c][...].astype(F32)

    def load_grad(k, start, lanes):
        rows = pl.ds(k * BLOCK + start, SLAB)
        return gg_ref[rows, lanes] * query_ref[rows, lanes].astype(F32)

    copies[0].wait()
    blocks_in(load_grad, signal, count, columns, ag_ref)
    copies[1].wait()
    copies[2].wait()
    for leaf in range(count):
        grads = dot(forward_table(tabs, leaf), ag_ref[leaf])
        table = inverse_table(tabs, leaf)
        ks = ks_ref[leaf].astype(F32)
        bx_ref[leaf] = dot(table, complex_product(ks, grads, True))
        xs = xs_ref[leaf].astype(F32)
        bk_ref[leaf] = dot(table, complex_product(xs, grads, True))
    copies[3].wait()
    copies[4].wait()
    gs_ref[:, seq_len:] = jnp.zeros((3, PAD, columns), F32)
    acc_ref[...] = jnp.zeros(acc_ref.shape, F32)

    def store_mixed(k, start, lanes, value):
        rows = pl.ds(k * BLOCK + start, SLAB)
        gg = gg_ref[rows, lanes]
        grad_conv = gg * query_ref[rows, lanes].astype(F32)
        first = pair_ref[0, rows, lanes].astype(F32)
        second = pair_ref[1, rows, lanes].astype(F32)
        grad_mixed = grad_conv * skip[:, lanes] + value
        gs_ref[0, rows, lanes] = gg * arg_ref[rows, lanes].astype(F32)
        gs_ref[1, rows, lanes] = grad_mixed * second
        gs_ref[2, rows, lanes] = grad_mixed * first
        acc_ref[13, :, lanes] += fold_rows(grad_conv * (first * second))

    blocks_out(store_mixed, signal, count, columns, bx_ref)
    gk_ref[0:PAD] = jnp.zeros((PAD, columns), F32)
    gk_ref[PAD + seq_len :] = jnp.zeros((PAD, columns), F32)

    def store_taps(k, start, lanes, value):
        pooled = three_sum(decayed_ref, k * BLOCK + start, SLAB, lanes)
        kept = jnp.where(jnp.abs(pooled) > CUT, value, 0.0)
        gk_ref[pl.ds(PAD + k * BLOCK + start, SLAB), lanes] = kept

    blocks_out(store_taps, filt, count, columns, bk_ref)

    shards, lines, width = gtaps_ref.shape

    def taps_body(shard, _):
        for group in range(width // columns):
            start = pl.multiple_of((shard * (width // columns) + group) * lines, lines)
            grad = three_sum(gk_ref, start, lines, slice(None))
            times = (lax.broadcasted_iota(jnp.int32, (lines, columns), 0) + start).astype(F32)
            low = (grad * decay_ref[pl.ds(start, lines)]).astype(BF16)
            gtaps_ref[shard, :, group * columns : (group + 1) * columns] = low
            acc_ref[12] -= fold_rows(times * grad * decayed_ref[pl.ds(PAD + start, lines)])
        return 0

    lax.fori_loop(0, shards, taps_body, 0)

    copies[5].wait()

    def short_block(block, target_ref, target, chunk, line):
        start = pl.multiple_of(block * BLOCK, BLOCK)
        inside = jnp.where(two_docs & (block == count // 2 - 1), 0.0, 1.0).astype(F32)
        for s in range(3):
            stream = streams_ref[s, pl.ds(start, BLOCK)].astype(F32)
            first = gs_ref[s, pl.ds(start, BLOCK)]
            beyond = gs_ref[s, pl.ds(start + BLOCK, PAD)] * inside
            window = jnp.concatenate([first, beyond], axis=0)
            acc_ref[s] += fold_rows(first * stream)
            total = short_ref[0, s : s + 1] * first
            for j in (1, 2):
                grad = window[j : j + BLOCK]
                acc_ref[3 * j + s] += fold_rows(grad * stream)
                total = total + short_ref[j, s : s + 1] * grad
            acc_ref[9 + s] += fold_rows(total)
            low = total.astype(BF16)
            target_ref[s, pl.ds(target, BLOCK)] = low
            if chunk is not None:
                lanes = slice(chunk * columns, (chunk + 1) * columns)
                packed_ref[s, pl.ds(line, BLOCK), lanes] = low

    for chunk in range(CHUNKS):

        def short_body(step, _):
            line = pl.multiple_of(step * BLOCK, BLOCK)
            first = chunk * (half_rows // CHUNKS) // BLOCK
            target = pl.multiple_of((step + first) * BLOCK, BLOCK)
            own_block = core * (count // 2) + first + step
            short_block(own_block, gst_own_ref, target, None, None)
            other_block = (1 - core) * (count // 2) + first + step
            short_block(other_block, gst_other_ref, target, chunk, line)
            return 0

        lax.fori_loop(0, count // 2 // CHUNKS, short_body, 0)

    sums_ref[...] = jnp.sum(acc_ref[...], axis=1)


def conv_backward(flags, own, other, query, arg, pair, streams, xs, ks, taps, rates, skip, short3, tabs):
    seq_len, channels = query.shape
    count = seq_len // BLOCK
    big = (query, ks, xs, arg, pair, streams)
    args = big + (taps, rates, skip, short3, *own, *other) + tabs
    spectrum = (count, 2 * BLOCK, channels)
    outs = [
        jax.ShapeDtypeStruct((3, seq_len // 2, channels), BF16),
        jax.ShapeDtypeStruct((3, seq_len // 2, channels), BF16),
        jax.ShapeDtypeStruct((3, seq_len // 2 // CHUNKS, CHUNKS * channels), BF16),
        jax.ShapeDtypeStruct(taps.shape, BF16),
        jax.ShapeDtypeStruct((16, channels), F32),
    ]
    padded = (seq_len + 2 * PAD, channels)
    return pl.pallas_call(
        conv_back_kernel,
        grid_spec=pltpu.PrefetchScalarGridSpec(
            num_scalar_prefetch=1,
            grid=(1,),
            in_specs=[ANYWHERE] * len(big) + [whole(item.shape) for item in args[len(big) :]],
            out_specs=[whole(item.shape) for item in outs],
            scratch_shapes=[
                pltpu.VMEM((seq_len, channels), F32),
                pltpu.VMEM(spectrum, BF16),
                pltpu.VMEM(spectrum, F32),
                pltpu.VMEM(spectrum, F32),
                pltpu.VMEM((3, seq_len + PAD, channels), F32),
                pltpu.VMEM(padded, F32),
                pltpu.VMEM((seq_len, channels), F32),
                pltpu.VMEM(padded, F32),
                pltpu.VMEM((16, 8, channels), F32),
            ]
            + [pltpu.VMEM(item.shape, item.dtype) for item in big]
            + [pltpu.SemaphoreType.DMA((len(big),))],
        ),
        out_shape=outs,
        compiler_params=limit(54),
        name="conv_backward",
        cost_estimate=cost(),
    )(flags, *args)


def cot_back_kernel(flags, cot_ref, down0_ref, down1_ref, dh0_ref, dh1_ref, sum_ref):
    cot = cot_ref[...]
    dh0_ref[...] = dot_rhs_t(cot, down0_ref[...]).astype(BF16)
    dh1_ref[...] = dot_rhs_t(cot, down1_ref[...]).astype(BF16)

    @pl.when(pl.program_id(0) == 0)
    def _():
        sum_ref[...] = jnp.zeros(sum_ref.shape, F32)

    sum_ref[...] += fold_rows(cot.astype(F32))


def cot_back(flags, cot, down0, down1):
    seq_len, width = cot.shape
    units = down0.shape[0]
    steps = seq_len // 2 // TILE
    long = pl.BlockSpec((TILE, units), lambda i, f: (i, 0))
    return pl.pallas_call(
        cot_back_kernel,
        grid_spec=pltpu.PrefetchScalarGridSpec(
            num_scalar_prefetch=1,
            grid=(steps,),
            in_specs=[
                pl.BlockSpec((TILE, width), lambda i, f: (f[1] * steps + i, 0)),
                whole(down0.shape), whole(down0.shape),
            ],
            out_specs=[long, long, whole((8, width))],
        ),
        out_shape=[
            jax.ShapeDtypeStruct((seq_len // 2, units), BF16),
            jax.ShapeDtypeStruct((seq_len // 2, units), BF16),
            jax.ShapeDtypeStruct((8, width), F32),
        ],
        name="cot_back",
        compiler_params=limit(20),
        cost_estimate=cost(),
    )(flags, cot, down0, down1)


def mlp_kernel(
    chips, chunk, flags, tok_ref, bias_ref, gain_ref, shift_ref, dh0_ref, dh1_ref,
    up0_ref, up1_ref, bup_ref, down0_ref, down1_ref, *refs
):
    gated_refs, po_refs = refs[: 2 * chips], refs[2 * chips : 4 * chips]
    hid_ref, normed_ref, act0_ref, act1_ref, gp0_ref, gp1_ref, out_ref, gn_ref, sum_ref = refs[-9:]
    step = pl.program_id(0)
    channels = po_refs[0].shape[0]
    mine = (slice(None), slice(chunk * channels, (chunk + 1) * channels))

    def from_chip(items, chip, core, where):
        value = items[core][where]
        for distance in range(1, chips):
            there = lax.rem(flags[2] + distance, chips) == chip
            value = jnp.where(there, items[2 * distance + core][where], value)
        return value

    attn = None
    for chip in range(chips):
        for core in range(2):
            term = dot(
                from_chip(gated_refs, chip, core, mine), from_chip(po_refs, chip, core, ...)
            )
            attn = term if attn is None else attn + term
    hidden_one = tok_ref[...].astype(F32) + (attn + bias_ref[...])
    hid_ref[...] = hidden_one
    unit, _ = normalize(hidden_one)
    normed = (unit * gain_ref[...] + shift_ref[...]).astype(BF16)
    normed_ref[...] = normed
    out_total = grad_total = None

    @pl.when(step == 0)
    def _():
        sum_ref[...] = jnp.zeros(sum_ref.shape, F32)

    for j, (up_ref, down_ref, dh_ref, act_ref, gp_ref) in enumerate(
        (
            (up0_ref, down0_ref, dh0_ref, act0_ref, gp0_ref),
            (up1_ref, down1_ref, dh1_ref, act1_ref, gp1_ref),
        )
    ):
        pre = dot(normed, up_ref[...]) + bup_ref[j : j + 1]
        cdf = 0.5 * (1.0 + lax.erf(pre * math.sqrt(0.5)))
        slope = cdf + pre * (jnp.exp(-0.5 * pre * pre) * (1.0 / math.sqrt(2.0 * math.pi)))
        act = (pre * cdf).astype(BF16)
        act_ref[...] = act
        out_part = dot(act, down_ref[...])
        grad_pre = (dh_ref[...].astype(F32) * slope).astype(BF16)
        gp_ref[...] = grad_pre
        sum_ref[j] += fold_rows(grad_pre.astype(F32))
        grad_part = dot_rhs_t(grad_pre, up_ref[...])
        out_total = out_part if j == 0 else out_total + out_part
        grad_total = grad_part if j == 0 else grad_total + grad_part
    out_ref[...] = out_total.astype(BF16)
    gn_ref[...] = grad_total.astype(BF16)


def mlp(flags, chunk, chunks, tokens, bias, gain, shift, dh0, dh1, up0, up1, bup, down0, down1, gated, po, carried):
    seq_len, width = tokens.shape
    units = up0.shape[1]
    half = seq_len // 2
    rows = half // chunks
    steps = rows // TILE

    def mine(i, flags):
        return (flags[1] * (chunks * steps) + chunk * steps + i, 0)

    def part(i, flags):
        return (chunk * steps + i, 0)

    def row(i, flags):
        return (i, 0)

    wide = pl.BlockSpec((TILE, width), part)
    long = pl.BlockSpec((TILE, units), part)
    fixed = (up0, up1, bup, down0, down1)
    args = (tokens, bias, gain, shift, dh0, dh1) + fixed + tuple(gated) + tuple(po)
    first = 1 + len(args)
    shared = [(width, F32), (width, BF16)] + [(units, BF16)] * 4 + [(width, BF16)]
    return pl.pallas_call(
        partial(mlp_kernel, len(gated) // 2, chunk),
        grid_spec=pltpu.PrefetchScalarGridSpec(
            num_scalar_prefetch=1,
            grid=(steps,),
            in_specs=[
                pl.BlockSpec((TILE, width), mine),
                whole((width,)), whole((width,)), whole((width,)), long, long,
            ]
            + [whole(item.shape) for item in fixed]
            + [pl.BlockSpec((TILE, item.shape[1]), row) for item in gated]
            + [whole(item.shape) for item in po]
            + [pl.BlockSpec(memory_space=pl.ANY) for _ in carried],
            out_specs=[wide, wide, long, long, long, long, wide]
            + [pl.BlockSpec((TILE, width), row), whole((2, 8, units))],
        ),
        out_shape=[jax.ShapeDtypeStruct((half, size), kind) for size, kind in shared]
        + [jax.ShapeDtypeStruct((rows, width), BF16), jax.ShapeDtypeStruct((2, 8, units), F32)],
        input_output_aliases={first + k: k for k in range(len(carried))},
        name="mlp",
        compiler_params=limit(24),
        cost_estimate=cost(),
    )(flags, *args, *carried)


def mlp_back_kernel(
    chunk, flags, hid_ref, own_ref, recv_ref, cot_ref, gain_ref, po0_ref, po1_ref, g0_ref, g1_ref, *refs
):
    gh_ref, gg0_ref, gg1_ref, kept_ref, sent_ref, low_ref, sum_ref = refs[-7:]
    step = pl.program_id(0)
    channels = po0_ref.shape[0]
    lanes = slice(chunk * channels, (chunk + 1) * channels)
    unit, rate = normalize(hid_ref[...])
    grad = own_ref[...].astype(F32) + recv_ref[...].astype(F32)
    grad_hidden = cot_ref[...].astype(F32) + norm_back(grad, unit, rate, gain_ref[...])
    gh_ref[...] = grad_hidden
    low = grad_hidden.astype(BF16)
    gg0_ref[...] = dot_rhs_t(low, po0_ref[...]).astype(BF16)
    gg1_ref[...] = dot_rhs_t(low, po1_ref[...]).astype(BF16)

    @pl.when(step == 0)
    def _():
        for k, ref in enumerate((kept_ref, sent_ref, sum_ref)):
            ref[...] = refs[k][...] if chunk else jnp.zeros(ref.shape, F32)

    sum_ref[0] += fold_rows(grad * unit)
    sum_ref[1] += fold_rows(grad)
    sum_ref[2] += fold_rows(grad_hidden)
    kept_ref[...] += dot_lhs_t(g0_ref[:, lanes], low)
    sent_ref[...] += dot_lhs_t(g1_ref[:, lanes], low)

    @pl.when(step == pl.num_programs(0) - 1)
    def _():
        low_ref[...] = sent_ref[...].astype(BF16)


def mlp_back(flags, chunk, chunks, hid, own, recv, cot, gain, po0, po1, g0, g1, carried):
    rows, width = own.shape
    channels = po0.shape[0]
    steps = rows // TILE

    def mine(i, flags):
        return (flags[1] * (chunks * steps) + chunk * steps + i, 0)

    def row(i, flags):
        return (i, 0)

    wide = pl.BlockSpec((TILE, width), row)
    thin = pl.BlockSpec((TILE, channels), row)
    packed = pl.BlockSpec((TILE, g0.shape[1]), row)
    return pl.pallas_call(
        partial(mlp_back_kernel, chunk),
        grid_spec=pltpu.PrefetchScalarGridSpec(
            num_scalar_prefetch=1,
            grid=(steps,),
            in_specs=[
                pl.BlockSpec((TILE, width), lambda i, f: (chunk * steps + i, 0)),
                wide, wide, pl.BlockSpec((TILE, width), mine),
                whole((width,)), whole(po0.shape), whole(po0.shape), packed, packed,
            ]
            + [whole(item.shape) for item in carried],
            out_specs=[wide, thin, thin]
            + [whole((channels, width))] * 3
            + [whole((3, 8, width))],
        ),
        out_shape=[
            jax.ShapeDtypeStruct((rows, width), F32),
            jax.ShapeDtypeStruct((rows, channels), BF16),
            jax.ShapeDtypeStruct((rows, channels), BF16),
            jax.ShapeDtypeStruct((channels, width), F32),
            jax.ShapeDtypeStruct((channels, width), F32),
            jax.ShapeDtypeStruct((channels, width), BF16),
            jax.ShapeDtypeStruct((3, 8, width), F32),
        ],
        name="mlp_back",
        compiler_params=limit(20),
        cost_estimate=cost(30 if chunk else 0),
    )(flags, hid, own, recv, cot, gain, po0, po1, g0, g1, *carried)


def mlp_grads_kernel(
    flags, act0_ref, act1_ref, norm_ref, cot_ref, gp0_ref, gp1_ref, kept_ref, sent_ref
):
    shards, rows, _ = kept_ref.shape
    rows = rows // 2

    def put(ref, first, lhs_ref, rhs_ref):
        grad = dot_lhs_t(lhs_ref[...], rhs_ref[...]).astype(ref.dtype)
        for k in range(shards):
            ref[k, first : first + rows] = grad[k * rows : (k + 1) * rows]

    put(sent_ref, 0, act1_ref, cot_ref)
    put(sent_ref, rows, gp1_ref, norm_ref)
    put(kept_ref, 0, act0_ref, cot_ref)
    put(kept_ref, rows, gp0_ref, norm_ref)


def mlp_grads(flags, shards, act0, act1, normed, cot, gp0, gp1):
    half, units = act0.shape
    width = normed.shape[1]
    steps = 2 if units // 2 % 128 == 0 else 1
    lines = 2 * units // shards
    out = pl.BlockSpec((shards // steps, lines, width), lambda i, f: (i, 0, 0))
    part = pl.BlockSpec((half, units // steps), lambda i, f: (0, i))
    return pl.pallas_call(
        mlp_grads_kernel,
        grid_spec=pltpu.PrefetchScalarGridSpec(
            num_scalar_prefetch=1,
            grid=(steps,),
            in_specs=[
                part, part, whole(normed.shape),
                pl.BlockSpec((half, width), lambda i, f: (f[1], 0)), part, part,
            ],
            out_specs=[out, out],
        ),
        out_shape=[jax.ShapeDtypeStruct((shards, lines, width), kind) for kind in (F32, BF16)],
        name="mlp_grads",
        compiler_params=limit(24),
        cost_estimate=cost(),
    )(flags, act0, act1, normed, cot, gp0, gp1)


def mixer_grads_kernel(
    flags, own_ref, send_ref, norm_ref, kept_ref, recv_ref, gtaps_ref, out_ref
):
    half = own_ref.shape[1]
    step = pl.program_id(0)
    shards, lines, _ = out_ref.shape
    rows = lines - gtaps_ref.shape[1]

    def put(grad):
        low = grad.astype(BF16)
        for k in range(shards):
            out_ref[k, 0:rows] = low[k * rows : (k + 1) * rows]

    @pl.when(step < 3)
    def _():
        put(
            dot_lhs_t(own_ref[0], norm_ref[0:half]) + dot_lhs_t(send_ref[0], norm_ref[half:])
        )

    @pl.when(step == 3)
    def _():
        put(kept_ref[...] + recv_ref[...].astype(F32))

    out_ref[:, rows:] = gtaps_ref[...]


def mixer_grads(flags, own, send, normed, kept, recv, gtaps):
    _, half, channels = own.shape
    seq_len, width = normed.shape
    shards, lines, _ = gtaps.shape
    rows = 4 * channels // shards
    stream = pl.BlockSpec((1, half, channels), lambda i, f: (jnp.minimum(i, 2), 0, 0))
    return pl.pallas_call(
        mixer_grads_kernel,
        grid_spec=pltpu.PrefetchScalarGridSpec(
            num_scalar_prefetch=1,
            grid=(4,),
            in_specs=[
                stream, stream, whole(normed.shape), whole(kept.shape), whole(recv.shape),
                pl.BlockSpec((shards // 4, lines, width), lambda i, f: (i, 0, 0)),
            ],
            out_specs=pl.BlockSpec((shards // 4, rows + lines, width), lambda i, f: (i, 0, 0)),
        ),
        out_shape=jax.ShapeDtypeStruct((shards, rows + lines, width), BF16),
        name="mixer_grads",
        cost_estimate=cost(),
    )(flags, own, send, normed, kept, recv, gtaps)


def streams_back_kernel(chunk, flags, g0_ref, g1_ref, w0_ref, w1_ref, tok_ref, gn_ref, sum_ref):
    total = None
    columns = g0_ref.shape[2]
    lanes = slice(chunk * columns, (chunk + 1) * columns)
    for item, w_ref in (
        (lambda s: g0_ref[s], w0_ref), (lambda s: g1_ref[s, :, lanes], w1_ref)
    ):
        for s in range(3):
            term = dot(item(s), w_ref[s])
            total = term if total is None else total + term
    low = total.astype(BF16)
    gn_ref[...] = low
    part = low.astype(F32)
    unit, _ = normalize(tok_ref[...].astype(F32))

    @pl.when(pl.program_id(0) == 0)
    def _():
        sum_ref[...] = jnp.zeros(sum_ref.shape, F32)

    sum_ref[0] += fold_rows(part * unit)
    sum_ref[1] += fold_rows(part)


def streams_back(flags, chunk, chunks, g0, g1, w0, w1, tokens):
    width = tokens.shape[1]
    channels = g0.shape[2]
    rows = g0.shape[1] // chunks
    steps = rows // TILE
    half = chunks * steps
    part = pl.BlockSpec((3, TILE, channels), lambda i, f: (0, chunk * steps + i, 0))
    return pl.pallas_call(
        partial(streams_back_kernel, chunk),
        grid_spec=pltpu.PrefetchScalarGridSpec(
            num_scalar_prefetch=1,
            grid=(steps,),
            in_specs=[
                part,
                pl.BlockSpec((3, TILE, g1.shape[2]), lambda i, f: (0, i, 0)),
                whole(w0.shape), whole(w0.shape),
                pl.BlockSpec((TILE, width), lambda i, f: (f[1] * half + chunk * steps + i, 0)),
            ],
            out_specs=[pl.BlockSpec((TILE, width), lambda i, f: (i, 0)), whole((2, 8, width))],
        ),
        out_shape=[
            jax.ShapeDtypeStruct((rows, width), BF16),
            jax.ShapeDtypeStruct((2, 8, width), F32),
        ],
        name="streams_back",
        cost_estimate=cost(),
    )(flags, g0, g1, w0, w1, tokens)


def input_back_kernel(flags, tok_ref, own_ref, recv_ref, gain_ref, gh_ref, *refs):
    out_ref, send_ref = refs[-2:]
    unit, rate = normalize(tok_ref[...].astype(F32))
    grad = own_ref[...].astype(F32) + recv_ref[...].astype(F32)
    value = gh_ref[...] + norm_back(grad, unit, rate, gain_ref[...])
    out_ref[...] = value
    send_ref[...] = value


def input_back(flags, chunk, chunks, tokens, own, recv, gain, gh, whole_out):
    seq_len, width = tokens.shape
    rows = own.shape[0]
    steps = rows // TILE
    half = chunks * steps
    wide = pl.BlockSpec((TILE, width), lambda i, f: (i, 0))
    mine = pl.BlockSpec((TILE, width), lambda i, f: (f[1] * half + chunk * steps + i, 0))
    carried = [] if whole_out is None else [whole_out]
    return pl.pallas_call(
        input_back_kernel,
        grid_spec=pltpu.PrefetchScalarGridSpec(
            num_scalar_prefetch=1,
            grid=(steps,),
            in_specs=[mine, wide, wide, whole((width,)), wide]
            + [pl.BlockSpec(memory_space=pl.ANY) for _ in carried],
            out_specs=[mine, wide],
        ),
        out_shape=[
            jax.ShapeDtypeStruct((seq_len, width), F32),
            jax.ShapeDtypeStruct((rows, width), F32),
        ],
        input_output_aliases={6: 0} if carried else {},
        name="input_back",
        cost_estimate=cost(25 if chunk == chunks - 1 else 4),
    )(flags, tokens, own, recv, gain, gh, *carried)


def output_kernel(flags, hid_ref, own_ref, recv_ref, bias_ref, out_ref, send_ref):
    total = own_ref[...].astype(F32) + recv_ref[...].astype(F32)
    value = (hid_ref[...] + total + bias_ref[...]).astype(BF16)
    out_ref[...] = value
    send_ref[...] = value


def output_rows(flags, hid, own, recv, bias):
    half, width = own.shape
    steps = half // TILE
    wide = pl.BlockSpec((TILE, width), lambda i, f: (i, 0))
    return pl.pallas_call(
        output_kernel,
        grid_spec=pltpu.PrefetchScalarGridSpec(
            num_scalar_prefetch=1,
            grid=(steps,),
            in_specs=[wide, wide, wide, whole((width,))],
            out_specs=[pl.BlockSpec((TILE, width), lambda i, f: (f[1] * steps + i, 0)), wide],
        ),
        out_shape=[
            jax.ShapeDtypeStruct((2 * half, width), BF16),
            jax.ShapeDtypeStruct((half, width), BF16),
        ],
        name="output_rows",
        cost_estimate=cost(),
    )(flags, hid, own, recv, bias)


def after(value, *done):
    return lax.optimization_barrier((value,) + done)[0]


def swap_core(value, size):
    return lax.ppermute(value, "mp", [(i, i ^ 1) for i in range(size)])


def fetch(value, size, distance, across):
    pairs = [((i + 2 * distance) % size ^ across, i) for i in range(size)]
    return lax.ppermute(value, "mp", pairs)


def across_x(value, size):
    chips = size // 2
    if chips == 1:
        return value, jnp.zeros_like(value)
    if chips == 2:
        return value, fetch(value, size, 1, 0)
    terms = [value.astype(F32)]
    for distance in range(1, chips):
        terms.append(fetch(value, size, distance, 0).astype(F32))
    here = lax.axis_index("mp") // 2
    stacked = jnp.stack(terms)
    total = 0.0
    for chip in range(chips):
        total = total + lax.dynamic_index_in_dim(stacked, (chip - here) % chips, 0, keepdims=False)
    high = total.astype(BF16)
    return high, (total - high.astype(F32)).astype(BF16)


def dp_spread(value):
    return lax.all_to_all(value, "dp", 0, 0, tiled=True)


def dp_collect(value, size):
    return dp_spread(jnp.broadcast_to(value[None], (size,) + value.shape))


def dp_gather(value, size, order, begun=0):
    here = lax.axis_index("dp")
    bits = size.bit_length() - 1
    if not begun:
        value = value.reshape((1,) * bits + value.shape)
    for bit in order:
        axis = bits - 1 - bit
        other = lax.ppermute(value, "dp", [(i, i ^ (1 << bit)) for i in range(size)])
        side = (here >> bit) & 1
        value = jnp.where(
            side == 1,
            jnp.concatenate([other, value], axis),
            jnp.concatenate([value, other], axis),
        )
    return value


def joined(value, size):
    bits = size.bit_length() - 1
    rows = size * value.shape[bits]
    return value.reshape((rows,) + value.shape[bits + 1 :])


def per_device(
    dp, mp,
    tokens, lengths, mix_gain, mix_shift, proj_in, bias_in, short_taps, long_taps, decay_rates,
    skip_gain, proj_out, bias_out, mlp_gain, mlp_shift, proj_up, bias_up, proj_down, bias_down,
    cotangent,
):
    seq_len, width = tokens.shape
    channels = proj_in.shape[2]
    units = proj_up.shape[1]
    chips = mp // 2
    half = seq_len // 2
    core = (lax.axis_index("mp") % 2).astype(jnp.int32)
    chip = (lax.axis_index("mp") // 2).astype(jnp.int32)
    two_docs = (lengths[0, 0] < seq_len).astype(jnp.int32)
    flags = jnp.stack([two_docs, core, chip])
    swap = lambda value: swap_core(value, mp)
    tabs = tables(seq_len)

    shard = seq_len // dp
    fold = width // channels
    taps = long_taps.reshape(fold, shard // fold, channels).transpose(1, 0, 2)
    taps = dp_collect(taps.reshape(shard // fold, width), dp).reshape(dp, shard // fold, width)
    w3 = jnp.transpose(proj_in, (1, 2, 0))
    normed, streams, pair, query, mixed, xs = mixer_in(
        flags, tokens, mix_gain, mix_shift, w3, bias_in, short_taps, tabs
    )
    po = []
    out_weights = after(proj_out, mixed)
    for distance in range(chips):
        po.append(fetch(out_weights, mp, distance, 0) if distance else proj_out)
        po.append(fetch(out_weights, mp, distance, 1))
    down_other = swap(after(proj_down, mixed))
    own, other, arg, ks = conv_forward(
        flags, mixed, query, xs, taps, decay_rates, skip_gain, tabs
    )
    own, other = after(own, *po[1:], down_other), after(other, *po[1:], down_other)
    up_other = swap(after(proj_up, own))
    w3_other = swap(after(w3, own))
    bup = jnp.stack([bias_up, swap(after(bias_up, own))])
    gated = []
    for distance in range(chips):
        gated.append(fetch(own, mp, distance, 0) if distance else own)
        gated.append(fetch(other, mp, distance, 1))

    dh0, dh1, cot_sum = cot_back(flags, after(cotangent, own), proj_down, down_other)

    gnorms, bup_sum, carried = [], 0.0, []
    for c in range(CHUNKS):
        *carried, gnorm, bsum = mlp(
            flags, c, CHUNKS, tokens, bias_out, mlp_gain, mlp_shift, dh0, dh1,
            proj_up, up_other, bup, proj_down, down_other, gated, po, carried,
        )
        gnorms.append(across_x(gnorm, mp))
        bup_sum = bup_sum + bsum
    hid, normed_two, act0, act1, gp0, gp1, down = carried

    bup_sum = jnp.sum(bup_sum, axis=1)

    kept, sent = mlp_grads(flags, dp, act0, act1, normed_two, cotangent, gp0, gp1)
    received = swap(sent)

    gh, gg_own, gg_other, held = [], [], [], ()
    for c in range(CHUNKS):
        mine, recv = gnorms[c]
        last = c == CHUNKS - 1
        if last:
            down = after(down, recv)
        part = mlp_back(
            flags, c, CHUNKS, after(hid, kept), mine, recv, cotangent,
            mlp_gain, po[0], po[1], gated[0], gated[1], held,
        )
        gh.append(part[0])
        gg_own.append(part[1])
        gg_other.append(swap(part[2]))
        held = (part[3], part[4], part[6])
    po_kept, _, sums = held
    po_recv = swap(part[5])
    g_mlp = (kept + after(received, gg_own[-1]).astype(F32)).astype(BF16)
    query_back = after(query, g_mlp, po_recv)
    g_mlp = dp_spread(g_mlp)
    down, down_recv = across_x(down, mp)

    gst_own, gst_send, packed, g_taps, conv_sums = conv_backward(
        flags, gg_own, gg_other, query_back, arg, pair, streams, xs, ks, taps, decay_rates,
        skip_gain, short_taps, tabs,
    )
    gst_recv = swap(packed)
    bits = dp.bit_length() - 1

    g_in = mixer_grads(flags, gst_own, gst_send, normed, po_kept, po_recv, g_taps)
    gst = after(gst_own, g_in, down_recv)
    finals, norm_sums = [], 0.0
    for c in range(CHUNKS):
        gnorm, part = streams_back(flags, c, CHUNKS, gst, gst_recv, w3, w3_other, tokens)
        finals.append(across_x(gnorm, mp))
        norm_sums = norm_sums + part
        gst = after(gst, gnorm)
    orders = (list(range(bits))[::-1], [0] + list(range(1, bits))[::-1])
    output, send = output_rows(flags, after(hid, gnorm), down, down_recv, bias_down)
    g_mlp = after(g_mlp, send)
    spread = dp_spread(after(g_in, g_mlp))
    g_mlp = jnp.sum(g_mlp.astype(F32).reshape(dp, -1, width), axis=0).astype(BF16)
    g_down, g_up = jnp.split(g_mlp, 2, axis=0)
    input_grad = None
    sends = []
    gate = (send,)
    for c in range(CHUNKS):
        mine, recv = finals[c]
        input_grad, part = input_back(
            flags, c, CHUNKS, tokens, mine, recv, mix_gain, after(gh[c], *gate), input_grad
        )
        if c == 0:
            g_down = dp_gather(g_down, dp, orders[0][:1], 0)
            g_up = dp_gather(g_up, dp, orders[1][:1], 0)
            gate = (part, g_down, g_up)
        sends.append(swap(part))
    spread = after(spread, part)

    g_down = dp_gather(g_down, dp, orders[0][1:2], 1)
    g_up = dp_gather(g_up, dp, orders[1][1:2], 1)
    spread = after(spread, g_down, g_up)
    g_down = joined(dp_gather(g_down, dp, orders[0][2:], 2), dp).astype(F32)
    g_up = joined(dp_gather(g_up, dp, orders[1][2:], 2), dp)
    g_up = jnp.transpose(g_up).astype(F32)

    rows_in = 4 * channels // dp
    spread = jnp.sum(spread.astype(F32).reshape(dp, -1, width), axis=0)
    g_taps = spread[rows_in:].reshape(shard // fold, fold, channels)
    g_taps = g_taps.transpose(1, 0, 2).reshape(shard, channels)

    norm_sums = jnp.sum(after(norm_sums, part), axis=1)
    total_x = norm_sums
    for distance in range(1, chips):
        total_x = total_x + fetch(norm_sums, mp, distance, 0)
    shared = jnp.concatenate(
        [total_x, jnp.sum(sums, axis=1), jnp.sum(cot_sum, axis=0, keepdims=True)], axis=0
    )
    mine = jnp.concatenate([shared.reshape(-1), bup_sum[0]])
    theirs = swap(jnp.concatenate([shared.reshape(-1), bup_sum[1]]))
    small = jnp.concatenate([mine + theirs, conv_sums[:14].reshape(-1)])
    length = small.shape[0]
    lines = -(-length // (16 * width)) * 16
    small = jnp.pad(small, (0, lines * width - length)).reshape(lines, width)
    packed = jnp.concatenate([spread[:rows_in], small], axis=0).astype(BF16)
    packed = dp_collect(packed, dp).reshape(dp, -1, width)
    g_in = packed[:, :rows_in].reshape(4, channels, width)
    small = jnp.sum(packed[:, rows_in:].astype(F32), axis=0).reshape(-1)
    g_po = g_in[3].astype(F32)
    g_in = jnp.transpose(g_in[:3], (2, 0, 1)).astype(F32)
    shared = small[: 6 * width].reshape(6, width)
    g_bias_up = small[6 * width : 6 * width + units]
    conv_sums = small[6 * width + units : length].reshape(14, channels)

    def place(rows, whole_out, first):
        start = (1 - core) * half + first
        return lax.dynamic_update_slice_in_dim(whole_out, rows, start, 0)

    for c in range(CHUNKS):
        input_grad = place(sends[c], input_grad, c * (half // CHUNKS))
    output = place(swap(send), output, 0)

    return (
        output,
        input_grad,
        shared[0],
        shared[1],
        g_in,
        conv_sums[9:12],
        conv_sums[:9].reshape(3, 3, channels),
        g_taps,
        conv_sums[12],
        conv_sums[13],
        g_po,
        shared[4],
        shared[2],
        shared[3],
        g_up,
        g_bias_up,
        g_down,
        shared[5],
    )


def solution(mesh):
    in_specs = (
        P("dp", None), P("dp", None), P(), P(), P(None, None, "mp"), P(None, "mp"),
        P(None, None, "mp"), P("dp", "mp"), P("mp"), P("mp"), P("mp", None), P(), P(), P(),
        P(None, "mp"), P("mp"), P("mp", None), P(), P("dp", None),
    )
    out_specs = (
        P("dp", None), P("dp", None), P(), P(), P(None, None, "mp"), P(None, "mp"),
        P(None, None, "mp"), P("dp", "mp"), P("mp"), P("mp"), P("mp", None), P(), P(), P(),
        P(None, "mp"), P("mp"), P("mp", None), P(),
    )
    body = partial(per_device, mesh.shape["dp"], mesh.shape["mp"])
    return jax.shard_map(
        body, mesh=mesh, in_specs=in_specs, out_specs=out_specs, check_vma=False
    )
```
